128 devices in a mesh: slot: 16 (over y, z), head: 2 (over x_lo), conv: 4 (over x_hi, core).
Axes of the slice: x: 4 (x_hi: 2, x_lo: 2; x = x_hi * 2 + x_lo), y: 4, z: 4, core: 2. Of those that a mesh axis runs over, the one named last changes fastest.
Arguments:
- queries: bfloat16 [1024, 64, 128], P(('conv', 'slot'), 'head'), may hold values from -96 to 96
- out_grad: bfloat16 [1024, 64, 128], P(('conv', 'slot'), 'head'), may hold values from -768 to 768
- row_positions: int32 [1024], P('conv'), may hold values from 0 to 8191
- slot_offsets: int32 [16384], P('slot'), may hold values from 0 to 16382, as said below
- cache: float32 [2, 16384, 4, 128], P(None, 'slot', 'head'), may hold values from -12 to 12
- first_moment: float32 [2, 16384, 4, 128], P(None, 'slot', 'head'), may hold values from -6 to 6
- second_moment: float32 [2, 16384, 4, 128], P(None, 'slot', 'head'), may hold values from 0.01 to 1000
Outputs:
- new_cache: float32 [2, 16384, 4, 128], P(None, 'slot', 'head')
- new_first_moment: float32 [2, 16384, 4, 128], P(None, 'slot', 'head')
- new_second_moment: float32 [2, 16384, 4, 128], P(None, 'slot', 'head')
- query_grad: float32 [1024, 64, 128], P(('conv', 'slot'), 'head')
The draws below stay inside these ranges and needn't reach their ends.
Inputs may be any that keep to these rules, and one draw needn't show every extreme that they name: `slot_offsets`: never falls from one slot to the next; its first two entries are 0.
All inputs are finite; a program needn't handle non-finite values.
Results may differ from the reference program's by a relative error of at most 0.012.
The reference program's roundings to bfloat16 on the way (of `score_grad` and `prob_half`) count: a program that leaves them out, or rounds other values in their place, can miss the bound.
Values may be sent and summed in bfloat16 or wider, within the bound.
A program may use at most 128 MiB of HBM per device.

```python
import math
import jax
import jax.numpy as jnp
from jax import lax

QH = 64
KVH = 4
HD = 128
SLOT_DEV = 1024
STEP = 20
SLOTS = 16384
ROWS = 1024
N_SLOT = 16


def draw_cache(key, part):
    full_shape = (2, SLOTS, KVH, HD)
    centre = jax.random.normal(jax.random.fold_in(key, 12), (2, 1, KVH, HD), jnp.float32) * 0.7
    drawn = jnp.clip(jax.random.normal(jax.random.fold_in(key, 11), full_shape, jnp.float32), -5.0, 5.0) + centre
    return drawn


def draw_queries(key, part):
    full_shape = (ROWS, QH, HD)
    drawn = jnp.clip(jax.random.normal(jax.random.fold_in(key, 21), full_shape, jnp.float32), -5.0, 5.0)
    return drawn.astype(jnp.bfloat16)


def draw_slot_offsets(key, part):
    increments = jax.random.randint(jax.random.fold_in(key, 31), (SLOTS,), 0, 2)
    increments = increments * (jnp.arange(SLOTS) >= 2).astype(jnp.int32)
    offsets = jnp.cumsum(increments).astype(jnp.int32)
    return offsets.at[SLOTS - 1].set(jnp.int32(SLOTS - 2))


def set_ends(values, own_key, low, high):
    shape = values.shape
    index_at = [jax.random.randint(jax.random.fold_in(own_key, axis), (), 0, shape[axis]) for axis in range(len(shape))]
    values = values.at[tuple(index_at)].set(low)
    longest = shape.index(max(shape))
    index_at[longest] = (index_at[longest] + 1) % shape[longest]
    return values.at[tuple(index_at)].set(high)


def block_levels(stream_key, dims, split, low, top_value):
    def one(axis_at, shards_of):
        heights = jax.random.uniform(jax.random.fold_in(jax.random.fold_in(stream_key, 6), axis_at), (shards_of,), jnp.float32, low / len(split), top_value / len(split))
        return jnp.repeat(jnp.exp(heights), dims[axis_at] // shards_of).reshape((-1,) + (1,) * (len(dims) - axis_at - 1))

    factor_of = one(*split[0])
    for cut in split[1:]:
        factor_of = factor_of * one(*cut)
    return factor_of


def normal_values(stream_key, shape, scale, bound, cuts=(), held_as=jnp.bfloat16):
    loudness = block_levels(stream_key, shape, cuts, -0.22, 0.18) if cuts else 1.0
    values = jax.random.normal(stream_key, shape, jnp.float32) * scale * loudness
    return jnp.minimum(jnp.maximum(values, -bound), bound).astype(held_as)


def setup_inputs(seed: int = 0) -> dict:
    seeds = jax.random.split(jax.random.key(seed), 8)
    queries = draw_queries(jax.random.fold_in(seeds[7], 71), 0)
    out_grad = normal_values(seeds[1], (ROWS, QH, HD), ((SLOT_DEV * N_SLOT) ** 0.5), 768.0, ((0, 64), (1, 2)))
    row_positions = set_ends(jax.random.randint(seeds[2], (ROWS,), 0, SLOT_DEV * N_SLOT // 2), jax.random.fold_in(seeds[2], 1), 0, (SLOT_DEV * N_SLOT // 2) - 1).astype(jnp.int32)
    slot_offsets = draw_slot_offsets(jax.random.fold_in(seeds[7], 71), 0)
    cache = draw_cache(jax.random.fold_in(seeds[7], 71), 0)
    first_moment = normal_values(seeds[5], (2, SLOTS, KVH, HD), 1.0, 6.0, ((1, 16), (2, 2)), jnp.float32)
    second_moment = jnp.clip(jnp.exp(math.log(1000.0) - 11.512925 * jax.random.uniform(seeds[6], (2, SLOTS, KVH, HD), jnp.float32) ** block_levels(seeds[6], (2, SLOTS, KVH, HD), ((1, 16), (2, 2)), -0.2, 0.2)), 0.01, 1000.0)
    return {"queries": queries, "out_grad": out_grad, "row_positions": row_positions, "slot_offsets": slot_offsets, "cache": cache, "first_moment": first_moment, "second_moment": second_moment}


learn_rate = 0.01
beta_one = 0.9
beta_two = 0.95
adam_eps = 1e-08
masked_score = -1e+30

def reference(queries, out_grad, row_positions, slot_offsets, cache, first_moment, second_moment):
    hi_prec = lax.Precision.HIGHEST
    group_heads = QH // KVH
    score_scale = 1.0 / math.sqrt(HD)
    key_float = lax.optimization_barrier(cache[0].astype(jnp.bfloat16)).astype(jnp.float32)
    value_float = lax.optimization_barrier(cache[1].astype(jnp.bfloat16)).astype(jnp.float32)
    block_rows = 16
    block_count = ROWS // block_rows
    query_blocks = queries.reshape(block_count, block_rows, KVH, group_heads, HD)
    grad_blocks = out_grad.reshape(block_count, block_rows, KVH, group_heads, HD)
    position_blocks = row_positions.reshape(block_count, block_rows)

    def block_step(running, inputs):
        key_grad, value_grad = running
        query_block, grad_block, position_block = inputs
        query_float = query_block.astype(jnp.float32)
        grad_float = grad_block.astype(jnp.float32)
        visible = (slot_offsets[None, :] <= position_block[:, None])[:, None, None, :]
        raw_score = jnp.einsum('rkgd,skd->rkgs', query_float, key_float, precision=hi_prec) * score_scale
        scores = jnp.where(visible, raw_score, masked_score)
        largest = lax.optimization_barrier(jnp.max(scores, axis=-1, keepdims=True))
        denominator = lax.optimization_barrier(jnp.sum(jnp.where(visible, jnp.exp(scores - largest), 0.0), axis=-1, keepdims=True))
        log_total = largest + jnp.log(denominator)
        probability = jnp.where(visible, jnp.exp(scores - log_total), 0.0)
        prob_grad = jnp.einsum('rkgd,skd->rkgs', grad_float, value_float, precision=hi_prec)
        row_sum = lax.optimization_barrier(jnp.sum(probability * prob_grad, axis=-1, keepdims=True))
        score_grad = lax.optimization_barrier((probability * (prob_grad - row_sum)).astype(jnp.bfloat16)).astype(jnp.float32)
        prob_half = lax.optimization_barrier(probability.astype(jnp.bfloat16)).astype(jnp.float32)
        value_grad = value_grad + jnp.einsum('rkgs,rkgd->skd', prob_half, grad_float, precision=hi_prec)
        key_grad = key_grad + jnp.einsum('rkgs,rkgd->skd', score_grad, query_float, precision=hi_prec) * score_scale
        query_part = jnp.einsum('rkgs,skd->rkgd', score_grad, key_float, precision=hi_prec) * score_scale
        return ((key_grad, value_grad), query_part.reshape(block_rows, QH, HD))
    empty_grad = jnp.zeros((SLOTS, KVH, HD), jnp.float32)
    (key_grad, value_grad), query_parts = lax.scan(block_step, (empty_grad, empty_grad), (query_blocks, grad_blocks, position_blocks))
    query_grad = query_parts.reshape(ROWS, QH, HD)
    slot_grad = jnp.stack([key_grad, value_grad])
    new_first = beta_one * first_moment + (1.0 - beta_one) * slot_grad
    new_second = beta_two * second_moment + (1.0 - beta_two) * slot_grad * slot_grad
    first_fix = 1.0 - beta_one ** STEP
    second_fix = 1.0 - beta_two ** STEP
    new_cache = cache - learn_rate * (new_first / first_fix) / (jnp.sqrt(new_second / second_fix) + adam_eps)
    return (new_cache, new_first, new_second, query_grad)
```

```python
import functools
import math

import jax
import jax.numpy as jnp
from jax import lax
from jax.experimental import pallas as pl
from jax.experimental.pallas import tpu as pltpu
from jax.sharding import PartitionSpec as P

STEP = 20

SIDE = 4
STATS_CHUNK = 256
GRADS_CHUNK = 512
REDUCE_LAG = 2

learn_rate = 0.01
beta_one = 0.9
beta_two = 0.95
adam_eps = 1e-08
masked_score = -1e30

MESH = pl.DeviceIdType.MESH
BF16 = jnp.bfloat16
F32 = jnp.float32


def nt(a, b):
    return lax.dot_general(a, b, (((1,), (1,)), ((), ())), preferred_element_type=F32)


def nn(a, b):
    return lax.dot_general(a, b, (((1,), (0,)), ((), ())), preferred_element_type=F32)


def lanes(column, width):
    return jnp.concatenate([column] * (width // column.shape[1]), axis=1)


def stats_pass(q, g, key_ref, value_ref, offset_ref, position, score_scale, chunk):
    width = q.shape[0]
    largest = jnp.full((8, width), masked_score, F32)
    total = jnp.zeros((8, width), F32)
    product = jnp.zeros((8, width), F32)
    for at in range(0, key_ref.shape[0], chunk):
        score = nt(key_ref[at : at + chunk], q)
        prob_grad = nt(value_ref[at : at + chunk], g)
        visible = lanes(offset_ref[at : at + chunk], width) <= position
        score = jnp.where(visible, score * score_scale, masked_score).reshape(chunk // 8, 8, width)
        now = jnp.maximum(largest, score.max(0))
        weight = jnp.exp2(score - now[None])
        fade = jnp.exp2(largest - now)
        total = total * fade + weight.sum(0)
        product = product * fade + (weight * prob_grad.reshape(chunk // 8, 8, width)).sum(0)
        largest = now
    top = largest.max(0, keepdims=True)
    fade = jnp.exp2(largest - top)
    return top, (total * fade).sum(0, keepdims=True), (product * fade).sum(0, keepdims=True)


def grad_pass(q, g, key_ref, value_ref, key_t_ref, offset_ref, position, log_total, row_sum, key_grad, value_grad, score_scale, chunk):
    width = q.shape[0]
    query_grad = jnp.zeros((q.shape[1], width), F32)
    for at in range(0, key_ref.shape[0], chunk):
        part = slice(at, at + chunk)
        score = nt(key_ref[part], q)
        prob_grad = nt(value_ref[part], g)
        visible = lanes(offset_ref[part], width) <= position
        probability = jnp.where(visible, jnp.exp2(score * score_scale - log_total), 0.0)
        score_grad = (probability * (prob_grad - row_sum)).astype(BF16)
        value_grad[part] += nn(probability.astype(BF16), g)
        key_grad[part] += nn(score_grad, q)
        query_grad = query_grad + nn(key_t_ref[:, part], score_grad)
    return query_grad


NEAR_FIRST = ((0, 0), (0, 1), (0, 3), (1, 0), (3, 0), (1, 1), (1, 3), (3, 1), (3, 3), (0, 2), (2, 0), (1, 2), (3, 2), (2, 1), (2, 3), (2, 2))
FAR_FIRST = ((2, 2), (2, 1), (1, 2), (2, 3), (3, 2), (1, 1), (1, 3), (3, 1), (3, 3), (2, 0), (0, 2), (1, 0), (3, 0), (0, 1), (0, 3), (0, 0))


def looked_up(table, at):
    found = jnp.int32(table[0])
    for i in range(1, len(table)):
        found = found + (table[i] - table[i - 1]) * jnp.where(at >= i, 1, 0)
    return found


def whole_kernel(
    scale,
    query_in,
    grad_in,
    position_ref,
    offset_ref,
    cache_in,
    slot_grad_out,
    query_grad_out,
    q_all,
    g_all,
    stage,
    key_ref,
    value_ref,
    key_t_ref,
    key_grad,
    value_grad,
    own_stats,
    stats_in,
    known,
    terms,
    far_one,
    near_one,
    far_two,
    near_two,
    core_out,
    core_in,
    chip_out,
    chip_in,
    total_out,
    total_in,
    load_sem,
    gather_send,
    gather_recv,
    stats_send,
    stats_recv,
    known_send,
    known_recv,
    reduce_send,
    far_one_recv,
    near_one_recv,
    far_two_recv,
    near_two_recv,
    conv_send,
    conv_recv,
):
    n_slot = SIDE * SIDE
    kv_count, slots, head_width = key_ref.shape
    group = q_all.shape[3]
    own_rows = q_all.shape[2]
    width = own_rows * group
    half_rows = own_rows // 2
    scale2 = scale * math.log2(math.e)
    me = lax.axis_index("slot")
    my_y, my_z = me // SIDE, me % SIDE
    conv = lax.axis_index("conv")
    core = conv % 2
    sibling = conv + 1 - 2 * core
    partner = (conv + 2) % 4

    def slot_at(y, z):
        return ((y + SIDE) % SIDE) * SIDE + (z + SIDE) % SIDE

    barrier = pltpu.get_barrier_semaphore()

    def greet(i, _):
        pl.semaphore_signal(barrier, inc=1, device_id={"slot": (me + i) % n_slot}, device_id_type=MESH)
        return 0

    lax.fori_loop(1, n_slot, greet, 0)
    pl.semaphore_signal(barrier, inc=1, device_id={"conv": sibling}, device_id_type=MESH)
    pl.semaphore_signal(barrier, inc=1, device_id={"conv": partner}, device_id_type=MESH)

    loads = []
    for i, (source, target) in enumerate(((query_in, q_all), (grad_in, g_all))):
        for k in range(kv_count):
            loads.append(pltpu.make_async_copy(source.at[:, k * group : (k + 1) * group, :], target.at[k, me], load_sem.at[i, k]))
    cache_load = pltpu.make_async_copy(cache_in, stage, load_sem.at[2, 0])
    for load in loads:
        load.start()
    cache_load.start()
    for load in loads:
        load.wait()
    pl.semaphore_wait(barrier, n_slot + 1)

    def gather_copy(tensor, k, block, piece, device, sem_piece):
        buffer = (q_all, g_all)[tensor]
        view = buffer.at[k, block] if piece is None else buffer.at[k, block, pl.ds(piece * half_rows, half_rows)]
        return pltpu.make_async_remote_copy(
            src_ref=view,
            dst_ref=view,
            send_sem=gather_send.at[tensor, k],
            recv_sem=gather_recv.at[tensor, k, block, sem_piece],
            device_id={"slot": device},
            device_id_type=MESH,
        )

    def ring(tensor, first, step):
        along_y = (tensor == 0) == first
        return slot_at(my_y + step, my_z) if along_y else slot_at(my_y, my_z + step)

    def gather_own(k):
        for tensor in (0, 1):
            for first in (True, False):
                for step in (1, -1):
                    gather_copy(tensor, k, me, None, ring(tensor, first, step), 0).start()

    def gather_event(k, dy, dz):
        block = slot_at(my_y + dy, my_z + dz)
        for tensor in (0, 1):
            da, db = (dy, dz) if tensor == 0 else (dz, dy)
            halves = (db == 2) | ((db == 0) & (da == 2))
            own = (da == 0) & (db == 0)

            @pl.when(halves)
            def _():
                for piece in (0, 1):
                    gather_copy(tensor, k, block, piece, me, piece).wait_recv()

            @pl.when(jnp.logical_not(halves | own))
            def _():
                gather_copy(tensor, k, block, None, me, 0).wait_recv()

            @pl.when((db == 0) & (da == 3))
            def _():
                gather_copy(tensor, k, block, 0, ring(tensor, True, 1), 0).start()

            @pl.when((db == 0) & (da == 1))
            def _():
                gather_copy(tensor, k, block, 1, ring(tensor, True, -1), 1).start()

            @pl.when((db == 0) & (da != 0))
            def _():
                gather_copy(tensor, k, block, None, ring(tensor, False, 1), 0).start()
                gather_copy(tensor, k, block, None, ring(tensor, False, -1), 0).start()

            @pl.when(db == 3)
            def _():
                gather_copy(tensor, k, block, 0, ring(tensor, False, 1), 0).start()

            @pl.when(db == 1)
            def _():
                gather_copy(tensor, k, block, 1, ring(tensor, False, -1), 1).start()

    gather_own(0)

    cache_load.wait()
    for k in range(kv_count):
        key = stage[0, pl.ds(k, slots, stride=kv_count), :]
        key_ref[k] = key.astype(BF16)
        key_t_ref[k] = key.T.astype(BF16)
        value_ref[k] = stage[1, pl.ds(k, slots, stride=kv_count), :].astype(BF16)
    key_grad[...] = jnp.zeros_like(key_grad)
    value_grad[...] = jnp.zeros_like(value_grad)

    def all_slots(k, source, target, send_sem, recv_sem, own_source):
        def send(i, _):
            other = (me + i) % n_slot
            pltpu.make_async_remote_copy(
                src_ref=source.at[k, me if own_source else other],
                dst_ref=target.at[k, me],
                send_sem=send_sem.at[k],
                recv_sem=recv_sem.at[k],
                device_id={"slot": other},
                device_id_type=MESH,
            ).start()
            return 0

        lax.fori_loop(1, n_slot, send, 0)

    def wait_all(k, ref, sem):
        view = ref.at[k, pl.ds(0, n_slot - 1)]
        pltpu.make_async_copy(view, view, sem.at[k]).wait()

    def stats_out(k):
        all_slots(k, own_stats, stats_in, stats_send, stats_recv, False)

    def stats_combine(k):
        wait_all(k, stats_in, stats_recv)
        stats_in[k, me] = own_stats[k, me]
        every = stats_in[k]
        top = every[:, 0:2].max(0)
        fade = jnp.exp2(every[:, 0:2] - top[None])
        total = (every[:, 2:4] * fade).sum(0)
        row_sum = (every[:, 4:6] * fade).sum(0) / total
        known[k, me, 0:2] = top + jnp.log2(total)
        known[k, me, 2:4] = row_sum
        all_slots(k, known, known, known_send, known_recv, True)

    def rows_of(ref, k, block):
        return ref[k, block].reshape(width, head_width)

    def stats_step(t, _):
        k, at = t // n_slot, t % n_slot
        dy, dz = looked_up([d[0] for d in NEAR_FIRST], at), looked_up([d[1] for d in NEAR_FIRST], at)
        block = slot_at(my_y + dy, my_z + dz)

        @pl.when(t == n_slot)
        def _():
            stats_out(0)

        @pl.when(t == n_slot // 2)
        def _():
            gather_own(1)

        @pl.when(t == n_slot + 6)
        def _():
            stats_combine(0)

        gather_event(k, dy, dz)
        stats = stats_pass(
            rows_of(q_all, k, block),
            rows_of(g_all, k, block),
            key_ref.at[k],
            value_ref.at[k],
            offset_ref,
            position_ref[block],
            scale2,
            STATS_CHUNK,
        )
        for i, stat in enumerate(stats):
            for j in range(width // 128):
                row = i * (width // 128) + j
                own_stats[k, block, row : row + 1] = stat[:, j * 128 : (j + 1) * 128]
        return 0

    lax.fori_loop(0, kv_count * n_slot, stats_step, 0)
    stats_out(1)

    def reduce_copy(color, k, source, target, recv_sem, device):
        return pltpu.make_async_remote_copy(
            src_ref=source,
            dst_ref=target,
            send_sem=reduce_send.at[k, color],
            recv_sem=recv_sem,
            device_id={"slot": device},
            device_id_type=MESH,
        )

    quarter = head_width // 4

    def reduce_event(k, dy, dz):
        block = slot_at(my_y + dy, my_z + dz)
        for color in (0, 1):
            da, db = (dy, dz) if color == 0 else (dz, dy)
            a_at = ((my_y if color == 0 else my_z) + da) % SIDE
            mine = terms.at[k, color, block]

            def arrived(target, sem):
                pltpu.make_async_copy(target, target, sem).wait()
                return target[...].astype(F32)

            def add(rows, value):
                mine[rows] = (mine[rows].astype(F32) + value).astype(BF16)

            def pieces(target, sems, first, index):
                for side, step in ((0, 1), (1, -1)):
                    place = (k, color, side) + index
                    rows = mine.at[pl.ds(side * quarter, quarter)]
                    reduce_copy(color, k, rows, target.at[place], sems.at[place], ring(color, first, step)).start()

            def onward(target, sems, first, index, side):
                place = (k, color, side) + index
                reduce_copy(color, k, mine, target.at[place], sems.at[place], ring(color, first, 1 - 2 * side)).start()

            @pl.when(db == 2)
            def _():
                pieces(far_one, far_one_recv, False, (a_at,))

            for side, step in ((0, 1), (1, 3)):

                @pl.when(db == step)
                def _():
                    place = (k, color, side, a_at)
                    add(pl.ds(side * quarter, quarter), arrived(far_one.at[place], far_one_recv.at[place]))
                    onward(near_one, near_one_recv, False, (a_at,), side)

            @pl.when(db == 0)
            def _():
                total = mine[...].astype(F32)
                for side in (0, 1):
                    place = (k, color, side, a_at)
                    total = total + arrived(near_one.at[place], near_one_recv.at[place])
                mine[...] = total.astype(BF16)

                @pl.when(da == 2)
                def _():
                    pieces(far_two, far_two_recv, True, ())

                for side, step in ((0, 1), (1, 3)):

                    @pl.when(da == step)
                    def _():
                        place = (k, color, side)
                        add(pl.ds(side * quarter, quarter), arrived(far_two.at[place], far_two_recv.at[place]))
                        onward(near_two, near_two_recv, True, (), side)

    def reduce_end(k):
        sums = []
        for color in (0, 1):
            total = terms[k, color, me].astype(F32)
            for side in (0, 1):
                place = (k, color, side)
                view = near_two.at[place]
                pltpu.make_async_copy(view, view, near_two_recv.at[place]).wait()
                total = total + view[...].astype(F32)
            sums.append(total)
        rows = jnp.concatenate(sums, axis=0).T.reshape(own_rows, group, head_width)
        query_grad_out[:, k * group : (k + 1) * group, :] = rows

    half = slots // 2

    def conv_copy(source, target, place, device):
        return pltpu.make_async_remote_copy(
            src_ref=source,
            dst_ref=target,
            send_sem=conv_send.at[place],
            recv_sem=conv_recv.at[place],
            device_id={"conv": device},
            device_id_type=MESH,
        )

    def conv_one(k):
        theirs = pl.ds(pl.multiple_of((1 - core) * half, half), half)
        core_out[k, 0] = (key_grad[k, theirs, :] * scale).astype(BF16)
        core_out[k, 1] = value_grad[k, theirs, :].astype(BF16)
        conv_copy(core_out.at[k], core_in.at[k], (k, 0), sibling).start()

    def conv_two(k):
        conv_copy(core_out.at[k], core_in.at[k], (k, 0), sibling).wait_recv()
        ours = pl.ds(pl.multiple_of(core * half, half), half)
        chip_out[k, 0] = (key_grad[k, ours, :] * scale + core_in[k, 0].astype(F32)).astype(BF16)
        chip_out[k, 1] = (value_grad[k, ours, :] + core_in[k, 1].astype(F32)).astype(BF16)
        conv_copy(chip_out.at[k], chip_in.at[k], (k, 1), partner).start()

    def store_total(k, owner, value):
        for i in (0, 1):
            place = pl.ds(pl.multiple_of(owner * (half * kv_count), half * kv_count) + k, half, stride=kv_count)
            slot_grad_out[i, place, :] = value[i]

    def conv_three(k):
        conv_copy(chip_out.at[k], chip_in.at[k], (k, 1), partner).wait_recv()
        total_out[k] = (chip_out[k].astype(F32) + chip_in[k].astype(F32)).astype(BF16)
        conv_copy(total_out.at[k], total_in.at[k], (k, 2), sibling).start()
        store_total(k, core, total_out[k].astype(F32))

    def conv_end(k):
        conv_copy(total_out.at[k], total_in.at[k], (k, 2), sibling).wait_recv()
        store_total(k, 1 - core, total_in[k].astype(F32))
        for i in range(3):
            conv_copy(total_out.at[k], total_in.at[k], (k, i), sibling).wait_send()

    wait_all(0, known, known_recv)

    steps = kv_count * n_slot

    def order_at(t):
        at = t % n_slot
        return t // n_slot, looked_up([d[0] for d in FAR_FIRST], at), looked_up([d[1] for d in FAR_FIRST], at)

    def grads_step(t, _):
        @pl.when(t == 6)
        def _():
            stats_combine(1)

        @pl.when(t == n_slot)
        def _():
            wait_all(1, known, known_recv)
            conv_one(0)

        @pl.when(t == n_slot + 4)
        def _():
            conv_two(0)

        @pl.when(t == n_slot + 13)
        def _():
            conv_three(0)

        @pl.when(t >= REDUCE_LAG)
        def _():
            reduce_event(*order_at(t - REDUCE_LAG))

        @pl.when(t < steps)
        def _():
            k, dy, dz = order_at(t)
            block = slot_at(my_y + dy, my_z + dz)
            stats = known[k, block]
            both = [jnp.concatenate([stats[i : i + 1], stats[i + 1 : i + 2]], axis=1) for i in (0, 2)]
            found = grad_pass(
                rows_of(q_all, k, block),
                rows_of(g_all, k, block),
                key_ref.at[k],
                value_ref.at[k],
                key_t_ref.at[k],
                offset_ref,
                position_ref[block],
                both[0],
                both[1],
                key_grad.at[k],
                value_grad.at[k],
                scale2,
                GRADS_CHUNK,
            )
            found = (found * scale).astype(BF16)
            for color in (0, 1):
                terms[k, color, block] = found[color * head_width // 2 : (color + 1) * head_width // 2]

        @pl.when(t == steps)
        def _():
            conv_one(1)

        return 0

    lax.fori_loop(0, steps + REDUCE_LAG, grads_step, 0)
    conv_two(1)
    reduce_end(0)
    conv_end(0)
    reduce_end(1)
    conv_three(1)
    for k in range(kv_count):
        for tensor, buffer in enumerate((q_all, g_all)):
            view = buffer.at[k, pl.ds(0, n_slot - 1)]
            pltpu.make_async_copy(view, view, gather_send.at[tensor, k]).wait()
        wait_all(k, own_stats, stats_send)
        wait_all(k, known, known_send)
        for color in (0, 1):
            view = terms.at[k, color, pl.ds(0, n_slot - 1)]
            pltpu.make_async_copy(view, view, reduce_send.at[k, color]).wait()
    conv_end(1)


def local(queries, out_grad, row_positions, slot_offsets, cache, first_moment, second_moment):
    own_rows, head_count, head_width = queries.shape
    kv_count, slots = cache.shape[2], cache.shape[1]
    group = head_count // kv_count
    blocks = row_positions.shape[0] // own_rows
    width = own_rows * group
    scale = 1.0 / math.sqrt(head_width)

    offsets = jnp.broadcast_to(slot_offsets[:, None], (slots, 128))
    positions = jnp.repeat(row_positions, group).reshape(blocks, 1, width)
    flat = (2, slots * kv_count, head_width)

    vmem = pl.BlockSpec(memory_space=pltpu.VMEM)
    hbm = pl.BlockSpec(memory_space=pl.ANY)
    dma = pltpu.SemaphoreType.DMA
    rows_all = pltpu.VMEM((kv_count, blocks, own_rows, group, head_width), BF16)
    slots_half = pltpu.VMEM((kv_count, slots, head_width), BF16)
    slots_full = pltpu.VMEM((kv_count, slots, head_width), F32)
    stats = pltpu.VMEM((kv_count, blocks, 8, 128), F32)
    conv_half = pltpu.VMEM((kv_count, 2, slots // 2, head_width), BF16)
    slot_grad, query_grad = pl.pallas_call(
        functools.partial(whole_kernel, scale),
        out_shape=(jax.ShapeDtypeStruct(flat, F32), jax.ShapeDtypeStruct(queries.shape, F32)),
        in_specs=[hbm, hbm, vmem, vmem, hbm],
        out_specs=(vmem, vmem),
        scratch_shapes=[
            rows_all,
            rows_all,
            pltpu.VMEM(flat, F32),
            slots_half,
            slots_half,
            pltpu.VMEM((kv_count, head_width, slots), BF16),
            slots_full,
            slots_full,
            stats,
            stats,
            stats,
            pltpu.VMEM((kv_count, 2, blocks, head_width // 2, width), BF16),
            pltpu.VMEM((kv_count, 2, 2, SIDE, head_width // 4, width), BF16),
            pltpu.VMEM((kv_count, 2, 2, SIDE, head_width // 2, width), BF16),
            pltpu.VMEM((kv_count, 2, 2, head_width // 4, width), BF16),
            pltpu.VMEM((kv_count, 2, 2, head_width // 2, width), BF16),
        ]
        + [conv_half] * 6
        + [
            dma((3, kv_count)),
            dma((2, kv_count)),
            dma((2, kv_count, blocks, 2)),
            dma((kv_count,)),
            dma((kv_count,)),
            dma((kv_count,)),
            dma((kv_count,)),
            dma((kv_count, 2)),
            dma((kv_count, 2, 2, SIDE)),
            dma((kv_count, 2, 2, SIDE)),
            dma((kv_count, 2, 2)),
            dma((kv_count, 2, 2)),
            dma((kv_count, 3)),
            dma((kv_count, 3)),
        ],
        compiler_params=pltpu.CompilerParams(collective_id=0, has_side_effects=True, vmem_limit_bytes=48 << 20),
        name="whole",
    )(queries, out_grad, positions, offsets, cache.reshape(flat))

    first_flat, second_flat, cache_flat = (x.reshape(flat) for x in (first_moment, second_moment, cache))
    new_first = beta_one * first_flat + (1.0 - beta_one) * slot_grad
    new_second = beta_two * second_flat + (1.0 - beta_two) * slot_grad * slot_grad
    first_fix = 1.0 - beta_one**STEP
    second_fix = 1.0 - beta_two**STEP
    new_cache = cache_flat - learn_rate * (new_first / first_fix) / (jnp.sqrt(new_second / second_fix) + adam_eps)
    return tuple(x.reshape(cache.shape) for x in (new_cache, new_first, new_second)) + (query_grad,)


def solution(mesh):
    rows = P(("conv", "slot"), "head", None)
    slots = P(None, "slot", "head", None)
    return jax.shard_map(
        local,
        mesh=mesh,
        in_specs=(rows, rows, P("conv"), P("slot"), slots, slots, slots),
        out_specs=(slots, slots, slots, rows),
        check_vma=False,
    )
```

```python
import functools
import math

import jax
import jax.numpy as jnp
from jax import lax
from jax.experimental import pallas as pl
from jax.experimental.pallas import tpu as pltpu
from jax.sharding import PartitionSpec as P

STEP = 20

SIDE = 4
STATS_CHUNK = 256
GRADS_CHUNK = 256

learn_rate = 0.01
beta_one = 0.9
beta_two = 0.95
adam_eps = 1e-08
masked_score = -1e30

MESH = pl.DeviceIdType.MESH
BF16 = jnp.bfloat16
F32 = jnp.float32


def nt(a, b):
    return lax.dot_general(a, b, (((1,), (1,)), ((), ())), preferred_element_type=F32)


def nn(a, b):
    return lax.dot_general(a, b, (((1,), (0,)), ((), ())), preferred_element_type=F32)


def lanes(column, width):
    return jnp.concatenate([column] * (width // column.shape[1]), axis=1)


def stats_pass(q, g, key_ref, value_ref, offset_ref, position, score_scale, chunk):
    width = q.shape[0]
    largest = jnp.full((8, width), masked_score, F32)
    total = jnp.zeros((8, width), F32)
    product = jnp.zeros((8, width), F32)
    for at in range(0, key_ref.shape[0], chunk):
        score = nt(key_ref[at : at + chunk], q)
        prob_grad = nt(value_ref[at : at + chunk], g)
        visible = lanes(offset_ref[at : at + chunk], width) <= position
        score = jnp.where(visible, score * score_scale, masked_score).reshape(chunk // 8, 8, width)
        now = jnp.maximum(largest, score.max(0))
        weight = jnp.exp2(score - now[None])
        fade = jnp.exp2(largest - now)
        total = total * fade + weight.sum(0)
        product = product * fade + (weight * prob_grad.reshape(chunk // 8, 8, width)).sum(0)
        largest = now
    top = largest.max(0, keepdims=True)
    fade = jnp.exp2(largest - top)
    return top, (total * fade).sum(0, keepdims=True), (product * fade).sum(0, keepdims=True)


def grad_pass(q, g, key_ref, value_ref, key_t_ref, offset_ref, position, log_total, row_sum, key_grad, value_grad, score_scale, chunk):
    width = q.shape[0]
    query_grad = jnp.zeros((q.shape[1], width), F32)
    for at in range(0, key_ref.shape[0], chunk):
        part = slice(at, at + chunk)
        score = nt(key_ref[part], q)
        prob_grad = nt(value_ref[part], g)
        visible = lanes(offset_ref[part], width) <= position
        probability = jnp.where(visible, jnp.exp2(score * score_scale - log_total), 0.0)
        score_grad = (probability * (prob_grad - row_sum)).astype(BF16)
        value_grad[part] += nn(probability.astype(BF16), g)
        key_grad[part] += nn(score_grad, q)
        query_grad = query_grad + nn(key_t_ref[:, part], score_grad)
    return query_grad


NEAR_FIRST = ((0, 0), (0, 1), (0, 3), (1, 0), (3, 0), (0, 2), (2, 0), (1, 1), (1, 3), (3, 1), (3, 3), (2, 1), (2, 3), (1, 2), (3, 2), (2, 2))
FAR_FIRST = ((2, 2), (2, 1), (1, 2), (2, 3), (3, 2), (2, 0), (0, 2), (1, 1), (1, 3), (3, 1), (3, 3), (1, 0), (3, 0), (0, 1), (0, 3), (0, 0))
STEPS = (
    [(0, 0, p) for p in range(8)]
    + [(0, 1, p) for p in range(3)]
    + [(1, 0, p) for p in range(4)]
    + [(0, 1, p) for p in range(3, 8)]
    + [(1, 0, p) for p in range(4, 8)]
    + [(1, 1, p) for p in range(8)]
)
REDUCE = (
    ((0, 2, 2), (1, 2, 2), (1, 1, 2)),
    ((0, 1, 2), (1, 3, 2)),
    ((0, 3, 2), (0, 2, 1), (0, 2, 3), (1, 0, 2), (1, 2, 1), (1, 2, 3)),
    ((0, 0, 2), (0, 1, 1), (1, 1, 1)),
    ((0, 1, 3), (0, 3, 1), (0, 2, 0), (1, 1, 3), (1, 3, 1), (1, 2, 0)),
    ((0, 3, 3), (1, 3, 3), (1, 0, 1)),
    ((0, 0, 1), (0, 1, 0), (1, 0, 3), (1, 1, 0)),
    ((0, 0, 3), (0, 3, 0), (1, 3, 0)),
    (),
    ((0, 0, 0), (1, 0, 0)),
)
REDUCE_AT = ((13, 14, 15, 17, 21, 22, 23, 24, 25, 26), (25, 26, 27, 28, 29, 30, 31))


def looked_up(table, at):
    found = jnp.int32(table[0])
    for i in range(1, len(table)):
        if table[i] != table[i - 1]:
            found = found + (table[i] - table[i - 1]) * jnp.where(at >= i, 1, 0)
    return found


def whole_kernel(
    scale,
    query_in,
    grad_in,
    position_hbm,
    offset_hbm,
    cache_in,
    first_in,
    second_in,
    slot_grad_out,
    query_grad_out,
    stage,
    first_out,
    second_out,
    position_in,
    offset_in,
    position_ref,
    offset_ref,
    q_all,
    g_all,
    key_ref,
    value_ref,
    key_t_ref,
    key_grad,
    value_grad,
    own_stats,
    stats_in,
    known,
    terms,
    far_one,
    near_one,
    far_two,
    near_two,
    core_out,
    core_in,
    chip_out,
    chip_in,
    total_out,
    total_in,
    load_sem,
    gather_send,
    gather_recv,
    stats_send,
    stats_recv,
    known_send,
    known_recv,
    reduce_send,
    far_one_recv,
    near_one_recv,
    far_two_recv,
    near_two_recv,
    conv_send,
    conv_recv,
):
    n_slot = SIDE * SIDE
    kv_count, slots, head_width = key_ref.shape
    group = q_all.shape[3]
    own_rows = q_all.shape[2]
    width = own_rows * group
    scale2 = scale * math.log2(math.e)
    me = lax.axis_index("slot")
    my_y, my_z = me // SIDE, me % SIDE
    conv = lax.axis_index("conv")
    core = conv % 2
    sibling = conv + 1 - 2 * core
    partner = (conv + 2) % 4

    def slot_at(y, z):
        return ((y + SIDE) % SIDE) * SIDE + (z + SIDE) % SIDE

    barrier = pltpu.get_barrier_semaphore()

    def greet(i, _):
        pl.semaphore_signal(barrier, inc=1, device_id={"slot": (me + i) % n_slot}, device_id_type=MESH)
        return 0

    lax.fori_loop(1, n_slot, greet, 0)
    pl.semaphore_signal(barrier, inc=1, device_id={"conv": sibling}, device_id_type=MESH)
    pl.semaphore_signal(barrier, inc=1, device_id={"conv": partner}, device_id_type=MESH)

    loads = []
    for i, (source, target) in enumerate(((query_in, q_all), (grad_in, g_all))):
        for k in range(kv_count):
            loads.append(pltpu.make_async_copy(source.at[:, k * group : (k + 1) * group, :], target.at[k, me], load_sem.at[i, k]))
    moments = [pltpu.make_async_copy(x, y, load_sem.at[2, 1 + i]) for i, (x, y) in enumerate(((first_in, first_out), (second_in, second_out)))]
    cache_load = pltpu.make_async_copy(cache_in, stage, load_sem.at[2, 0])
    for load in loads:
        load.start()
    cache_load.start()
    small = [pltpu.make_async_copy(x, y, load_sem.at[i, 2]) for i, (x, y) in enumerate(((position_hbm, position_in), (offset_hbm, offset_in)))]
    for load in small:
        load.start()
    for load in loads:
        load.wait()

    pl.semaphore_wait(barrier, n_slot + 1)

    def gather_copy(tensor, k, block, device):
        view = (q_all, g_all)[tensor].at[k, block]
        return pltpu.make_async_remote_copy(
            src_ref=view,
            dst_ref=view,
            send_sem=gather_send.at[tensor, k],
            recv_sem=gather_recv.at[tensor, k, block],
            device_id={"slot": device},
            device_id_type=MESH,
        )

    def ring(tensor, first, step):
        along_y = (tensor == 0) == first
        return slot_at(my_y + step, my_z) if along_y else slot_at(my_y, my_z + step)

    def gather_own(k):
        for first in (True, False):
            for tensor in (0, 1):
                for step in (1, -1, 2):
                    gather_copy(tensor, k, me, ring(tensor, first, step)).start()

    def gather_turn(k):
        for step in (1, -1, 2):
            for tensor in (0, 1):
                gather_copy(tensor, k, ring(tensor, True, step), me).wait_recv()

    def gather_relay(k):
        for step in (1, -1, 2):
            for tensor in (0, 1):
                block = ring(tensor, True, step)
                for onward in (1, -1, 2):
                    gather_copy(tensor, k, block, ring(tensor, False, onward)).start()

    def gather_wait(k, dy, dz):
        for tensor, last in ((0, dz), (1, dy)):
            if last != 0:
                gather_copy(tensor, k, slot_at(my_y + dy, my_z + dz), me).wait_recv()

    gather_own(0)
    for load in moments:
        load.start()
    for load in small + [cache_load]:
        load.wait()
    for k in range(kv_count):
        key = stage[0, pl.ds(k, slots, stride=kv_count), :]
        key_ref[k] = key.astype(BF16)
        key_t_ref[k] = key.T.astype(BF16)
        value_ref[k] = stage[1, pl.ds(k, slots, stride=kv_count), :].astype(BF16)
    key_grad[...] = jnp.zeros_like(key_grad)
    value_grad[...] = jnp.zeros_like(value_grad)
    for i in range(slots // 128):
        row = offset_in[i : i + 1].astype(F32)
        offset_ref[i * 128 : (i + 1) * 128] = jnp.broadcast_to(row, (128, 128)).T
    spread = lax.broadcasted_iota(jnp.int32, (own_rows, width), 1) // group == lax.broadcasted_iota(jnp.int32, (own_rows, width), 0)
    for i in range(n_slot * own_rows // 128):
        rows = jnp.broadcast_to(position_in[i : i + 1].astype(F32), (128, 128)).T
        for j in range(128 // own_rows):
            mine = lanes(rows[j * own_rows : (j + 1) * own_rows], width)
            position_ref[i * (128 // own_rows) + j] = jnp.where(spread, mine, 0.0).sum(0, keepdims=True)

    def all_slots(k, source, target, send_sem, recv_sem, own_source):
        def send(i, _):
            other = (me + i) % n_slot
            pltpu.make_async_remote_copy(
                src_ref=source.at[k, me if own_source else other],
                dst_ref=target.at[k, me],
                send_sem=send_sem.at[k],
                recv_sem=recv_sem.at[k],
                device_id={"slot": other},
                device_id_type=MESH,
            ).start()
            return 0

        lax.fori_loop(1, n_slot, send, 0)

    def wait_all(k, ref, sem):
        view = ref.at[k, pl.ds(0, n_slot - 1)]
        pltpu.make_async_copy(view, view, sem.at[k]).wait()

    def stats_out(k):
        all_slots(k, own_stats, stats_in, stats_send, stats_recv, False)

    def stats_combine(k):
        wait_all(k, stats_in, stats_recv)
        stats_in[k, me] = own_stats[k, me]
        every = stats_in[k]
        top = every[:, 0:2].max(0)
        fade = jnp.exp2(every[:, 0:2] - top[None])
        total = (every[:, 2:4] * fade).sum(0)
        row_sum = (every[:, 4:6] * fade).sum(0) / total
        known[k, me, 0:2] = top + jnp.log2(total)
        known[k, me, 2:4] = row_sum
        all_slots(k, known, known, known_send, known_recv, True)

    def reduce_copy(color, k, source, target, recv_sem, device):
        return pltpu.make_async_remote_copy(
            src_ref=source,
            dst_ref=target,
            send_sem=reduce_send.at[k, color],
            recv_sem=recv_sem,
            device_id={"slot": device},
            device_id_type=MESH,
        )

    quarter = head_width // 4

    def reduce_event(k, color, da, db):
        dy, dz = (da, db) if color == 0 else (db, da)
        block = slot_at(my_y + dy, my_z + dz)
        a_at = ((my_y if color == 0 else my_z) + da) % SIDE
        mine = terms.at[k, color, block]

        def arrived(target, sem):
            pltpu.make_async_copy(target, target, sem).wait()
            return target[...].astype(F32)

        def add(side, target, sem):
            rows = pl.ds(side * quarter, quarter)
            mine[rows] = (mine[rows].astype(F32) + arrived(target, sem)).astype(BF16)

        def pieces(target, sems, first, index):
            for side, step in ((0, 1), (1, -1)):
                place = (k, color, side) + index
                rows = mine.at[pl.ds(side * quarter, quarter)]
                reduce_copy(color, k, rows, target.at[place], sems.at[place], ring(color, first, step)).start()

        def onward(target, sems, first, index, side):
            place = (k, color, side) + index
            reduce_copy(color, k, mine, target.at[place], sems.at[place], ring(color, first, 1 - 2 * side)).start()

        if db == 2:
            pieces(far_one, far_one_recv, False, (a_at,))
        elif db != 0:
            side = db // 2
            place = (k, color, side, a_at)
            add(side, far_one.at[place], far_one_recv.at[place])
            onward(near_one, near_one_recv, False, (a_at,), side)
        else:
            total = mine[...].astype(F32)
            for side in (0, 1):
                place = (k, color, side, a_at)
                total = total + arrived(near_one.at[place], near_one_recv.at[place])
            mine[...] = total.astype(BF16)
            if da == 2:
                pieces(far_two, far_two_recv, True, ())
            elif da != 0:
                side = da // 2
                place = (k, color, side)
                add(side, far_two.at[place], far_two_recv.at[place])
                onward(near_two, near_two_recv, True, (), side)

    def reduce_stage(k, stage):
        for event in REDUCE[stage]:
            reduce_event(k, *event)

    def reduce_end(k):
        sums = []
        for color in (0, 1):
            total = terms[k, color, me].astype(F32)
            for side in (0, 1):
                place = (k, color, side)
                view = near_two.at[place]
                pltpu.make_async_copy(view, view, near_two_recv.at[place]).wait()
                total = total + view[...].astype(F32)
            sums.append(total)
        rows = jnp.concatenate(sums, axis=0).T.reshape(own_rows, group, head_width)
        query_grad_out[:, k * group : (k + 1) * group, :] = rows

    half = slots // 2

    def conv_copy(hop, k, i, device):
        source, target = ((core_out, core_in), (chip_out, chip_in), (total_out, total_in))[hop]
        return pltpu.make_async_remote_copy(
            src_ref=source.at[k, i],
            dst_ref=target.at[k, i],
            send_sem=conv_send.at[k, hop, i],
            recv_sem=conv_recv.at[k, hop, i],
            device_id={"conv": device},
            device_id_type=MESH,
        )

    def own_grad(k, i, owner):
        rows = pl.ds(pl.multiple_of(owner * half, half), half)
        return key_grad[k, rows, :] * scale if i == 0 else value_grad[k, rows, :]

    def store_total(k, i, owner, value):
        place = pl.ds(pl.multiple_of(owner * (half * kv_count), half * kv_count) + k, half, stride=kv_count)
        slot_grad_out[i, place, :] = value

    def conv_one(k):
        for i in (0, 1):
            core_out[k, i] = own_grad(k, i, 1 - core).astype(BF16)
            conv_copy(0, k, i, sibling).start()

    def conv_two(k):
        for i in (0, 1):
            conv_copy(0, k, i, sibling).wait_recv()
            chip_out[k, i] = (own_grad(k, i, core) + core_in[k, i].astype(F32)).astype(BF16)
            conv_copy(1, k, i, partner).start()

    def conv_three(k):
        for i in (0, 1):
            conv_copy(1, k, i, partner).wait_recv()
            total_out[k, i] = (chip_out[k, i].astype(F32) + chip_in[k, i].astype(F32)).astype(BF16)
            conv_copy(2, k, i, sibling).start()
            store_total(k, i, core, total_out[k, i].astype(F32))

    def conv_end(k):
        for i in (0, 1):
            conv_copy(2, k, i, sibling).wait_recv()
            store_total(k, i, 1 - core, total_in[k, i].astype(F32))
            for hop in range(3):
                conv_copy(hop, k, i, sibling).wait_send()

    def step(t, _):
        def at_step(at):
            return pl.when(t == at)

        for work, k, at in (
            (gather_turn, 0, 0),
            (gather_relay, 0, 0),
            (gather_own, 1, 0),
            (stats_out, 0, 8),
            (gather_turn, 1, 8),
            (stats_combine, 0, 11),
            (gather_relay, 1, 11),
            (stats_out, 1, 20),
            (stats_combine, 1, 22),
        ):

            @at_step(at)
            def _():
                work(k)

        for k, at in ((0, 11), (1, 24)):

            @at_step(at)
            def _():
                wait_all(k, known, known_recv)

        for at, (which, k, pair) in enumerate(STEPS):
            if which == 0:

                @at_step(at)
                def _():
                    for place in NEAR_FIRST[2 * pair : 2 * pair + 2]:
                        gather_wait(k, *place)

        for stage, at in enumerate(REDUCE_AT[0]):
            also = REDUCE_AT[1][stage] if stage < len(REDUCE_AT[1]) else at

            @pl.when((t == at) | (t == also))
            def _():
                reduce_stage(jnp.where(t == at, 0, 1), stage)

        for work, at in ((conv_one, 24), (conv_two, 26), (conv_three, 30)):

            @at_step(at)
            def _():
                work(0)

        which, k, pair = (looked_up([entry[i] for entry in STEPS], t) for i in range(3))

        def blocks_of(order):
            found = []
            for i in (0, 1):
                dy, dz = (looked_up([d[axis] for d in order[i::2]], pair) for axis in (0, 1))
                found.append(slot_at(my_y + dy, my_z + dz))
            return found

        def rows_of(ref, blocks):
            return jnp.concatenate([ref[k, block].reshape(width, head_width) for block in blocks], axis=0)

        def positions_of(blocks):
            return jnp.concatenate([position_ref[block] for block in blocks], axis=1)

        @pl.when(which == 0)
        def _():
            blocks = blocks_of(NEAR_FIRST)
            stats = stats_pass(
                rows_of(q_all, blocks),
                rows_of(g_all, blocks),
                key_ref.at[k],
                value_ref.at[k],
                offset_ref,
                positions_of(blocks),
                scale2,
                STATS_CHUNK,
            )
            for i, stat in enumerate(stats):
                for j in range(2 * width // 128):
                    row = i * (width // 128) + j % (width // 128)
                    own_stats[k, blocks[j * 128 // width], row : row + 1] = stat[:, j * 128 : (j + 1) * 128]

        @pl.when(which == 1)
        def _():
            blocks = blocks_of(FAR_FIRST)
            stats = [known[k, block] for block in blocks]
            both = [jnp.concatenate([stat[row : row + 1] for stat in stats for row in (i, i + 1)], axis=1) for i in (0, 2)]
            found = grad_pass(
                rows_of(q_all, blocks),
                rows_of(g_all, blocks),
                key_ref.at[k],
                value_ref.at[k],
                key_t_ref.at[k],
                offset_ref,
                positions_of(blocks),
                both[0],
                both[1],
                key_grad.at[k],
                value_grad.at[k],
                scale2,
                GRADS_CHUNK,
            )
            found = (found * scale).astype(BF16)
            for i, block in enumerate(blocks):
                for color in (0, 1):
                    terms[k, color, block] = found[color * head_width // 2 : (color + 1) * head_width // 2, i * width : (i + 1) * width]

        return 0

    lax.fori_loop(0, len(STEPS), step, 0)
    conv_one(1)
    reduce_stage(1, 7)
    conv_two(1)
    reduce_end(0)
    conv_end(0)
    reduce_stage(1, 8)
    reduce_stage(1, 9)
    conv_three(1)
    reduce_end(1)
    for k in range(kv_count):
        for tensor, buffer in enumerate((q_all, g_all)):
            view = buffer.at[k, pl.ds(0, n_slot - 1)]
            pltpu.make_async_copy(view, view, gather_send.at[tensor, k]).wait()
        wait_all(k, own_stats, stats_send)
        wait_all(k, known, known_send)
        for color in (0, 1):
            view = terms.at[k, color, pl.ds(0, n_slot - 1)]
            pltpu.make_async_copy(view, view, reduce_send.at[k, color]).wait()
    for load in moments:
        load.wait()
    conv_end(1)


def local(queries, out_grad, row_positions, slot_offsets, cache, first_moment, second_moment):
    own_rows, head_count, head_width = queries.shape
    kv_count, slots = cache.shape[2], cache.shape[1]
    group = head_count // kv_count
    blocks = row_positions.shape[0] // own_rows
    width = own_rows * group
    scale = 1.0 / math.sqrt(head_width)

    flat = (2, slots * kv_count, head_width)

    vmem = pl.BlockSpec(memory_space=pltpu.VMEM)
    hbm = pl.BlockSpec(memory_space=pltpu.HBM)
    dma = pltpu.SemaphoreType.DMA
    rows_all = pltpu.VMEM((kv_count, blocks, own_rows, group, head_width), BF16)
    in_hbm = lambda x: pltpu.with_memory_space_constraint(x, pltpu.HBM)
    slots_half = pltpu.VMEM((kv_count, slots, head_width), BF16)
    slots_full = pltpu.VMEM((kv_count, slots, head_width), F32)
    stats = pltpu.VMEM((kv_count, blocks, 8, 128), F32)
    conv_half = pltpu.VMEM((kv_count, 2, slots // 2, head_width), BF16)
    slot_grad, query_grad, cache_flat, first_flat, second_flat = pl.pallas_call(
        functools.partial(whole_kernel, scale),
        out_shape=(jax.ShapeDtypeStruct(flat, F32), jax.ShapeDtypeStruct(queries.shape, F32)) + (jax.ShapeDtypeStruct(flat, F32),) * 3,
        in_specs=[hbm] * 7,
        out_specs=(vmem,) * 5,
        scratch_shapes=[
            pltpu.VMEM((blocks * own_rows // 128, 128), jnp.int32),
            pltpu.VMEM((slots // 128, 128), jnp.int32),
            pltpu.VMEM((blocks, 1, width), F32),
            pltpu.VMEM((slots, 128), F32),
            rows_all,
            rows_all,
            slots_half,
            slots_half,
            pltpu.VMEM((kv_count, head_width, slots), BF16),
            slots_full,
            slots_full,
            stats,
            stats,
            stats,
            pltpu.VMEM((kv_count, 2, blocks, head_width // 2, width), BF16),
            pltpu.VMEM((kv_count, 2, 2, SIDE, head_width // 4, width), BF16),
            pltpu.VMEM((kv_count, 2, 2, SIDE, head_width // 2, width), BF16),
            pltpu.VMEM((kv_count, 2, 2, head_width // 4, width), BF16),
            pltpu.VMEM((kv_count, 2, 2, head_width // 2, width), BF16),
        ]
        + [conv_half] * 6
        + [
            dma((3, 4)),
            dma((2, kv_count)),
            dma((2, kv_count, blocks)),
            dma((kv_count,)),
            dma((kv_count,)),
            dma((kv_count,)),
            dma((kv_count,)),
            dma((kv_count, 2)),
            dma((kv_count, 2, 2, SIDE)),
            dma((kv_count, 2, 2, SIDE)),
            dma((kv_count, 2, 2)),
            dma((kv_count, 2, 2)),
            dma((kv_count, 3, 2)),
            dma((kv_count, 3, 2)),
        ],
        compiler_params=pltpu.CompilerParams(collective_id=0, has_side_effects=True, vmem_limit_bytes=34 << 20),
        name="whole",
    )(in_hbm(queries), in_hbm(out_grad), in_hbm(row_positions.reshape(-1, 128)), in_hbm(slot_offsets.reshape(-1, 128)), *(in_hbm(x.reshape(flat)) for x in (cache, first_moment, second_moment)))

    new_first = beta_one * first_flat + (1.0 - beta_one) * slot_grad
    new_second = beta_two * second_flat + (1.0 - beta_two) * slot_grad * slot_grad
    first_fix = 1.0 - beta_one**STEP
    second_fix = 1.0 - beta_two**STEP
    new_cache = cache_flat - learn_rate * (new_first / first_fix) / (jnp.sqrt(new_second / second_fix) + adam_eps)
    return tuple(x.reshape(cache.shape) for x in (new_cache, new_first, new_second)) + (query_grad,)


def solution(mesh):
    rows = P(("conv", "slot"), "head", None)
    slots = P(None, "slot", "head", None)
    return jax.shard_map(
        local,
        mesh=mesh,
        in_specs=(rows, rows, P("conv"), P("slot"), slots, slots, slots),
        out_specs=(slots, slots, slots, rows),
        check_vma=False,
    )
```

```python
import functools
import math

import jax
import jax.numpy as jnp
from jax import lax
from jax.experimental import pallas as pl
from jax.experimental.pallas import tpu as pltpu
from jax.sharding import PartitionSpec as P

STEP = 20

SIDE = 4
STATS_CHUNK = 256
GRADS_CHUNK = 256

learn_rate = 0.01
beta_one = 0.9
beta_two = 0.95
adam_eps = 1e-08
masked_score = -1e30

MESH = pl.DeviceIdType.MESH
BF16 = jnp.bfloat16
F32 = jnp.float32


def nt(a, b):
    return lax.dot_general(a, b, (((1,), (1,)), ((), ())), preferred_element_type=F32)


def nn(a, b):
    return lax.dot_general(a, b, (((1,), (0,)), ((), ())), preferred_element_type=F32)


def lanes(column, width):
    return jnp.concatenate([column] * (width // column.shape[1]), axis=1)


def stats_pass(q, g, key_ref, value_ref, offset_ref, position, score_scale, chunk):
    width = q.shape[0]
    largest = jnp.full((8, width), masked_score, F32)
    total = jnp.zeros((8, width), F32)
    product = jnp.zeros((8, width), F32)
    for at in range(0, key_ref.shape[0], chunk):
        score = nt(key_ref[at : at + chunk], q)
        prob_grad = nt(value_ref[at : at + chunk], g)
        visible = lanes(offset_ref[at : at + chunk], width) <= position
        score = jnp.where(visible, score * score_scale, masked_score).reshape(chunk // 8, 8, width)
        now = jnp.maximum(largest, score.max(0))
        weight = jnp.exp2(score - now[None])
        fade = jnp.exp2(largest - now)
        total = total * fade + weight.sum(0)
        product = product * fade + (weight * prob_grad.reshape(chunk // 8, 8, width)).sum(0)
        largest = now
    top = largest.max(0, keepdims=True)
    fade = jnp.exp2(largest - top)
    return top, (total * fade).sum(0, keepdims=True), (product * fade).sum(0, keepdims=True)


def grad_pass(q, g, key_ref, value_ref, key_t_ref, offset_ref, position, log_total, row_sum, key_grad, value_grad, score_scale, chunk):
    width = q.shape[0]
    query_grad = jnp.zeros((q.shape[1], width), F32)
    for at in range(0, key_ref.shape[0], chunk):
        part = slice(at, at + chunk)
        score = nt(key_ref[part], q)
        prob_grad = nt(value_ref[part], g)
        visible = lanes(offset_ref[part], width) <= position
        probability = jnp.where(visible, jnp.exp2(score * score_scale - log_total), 0.0)
        score_grad = (probability * (prob_grad - row_sum)).astype(BF16)
        value_grad[part] += nn(probability.astype(BF16), g)
        key_grad[part] += nn(score_grad, q)
        query_grad = query_grad + nn(key_t_ref[:, part], score_grad)
    return query_grad


NEAR_FIRST = ((0, 0), (0, 1), (0, 3), (1, 0), (3, 0), (0, 2), (2, 0), (1, 1), (1, 3), (3, 1), (3, 3), (2, 1), (2, 3), (1, 2), (3, 2), (2, 2))
FAR_FIRST = ((2, 2), (2, 1), (1, 2), (2, 3), (3, 2), (2, 0), (0, 2), (1, 1), (1, 3), (3, 1), (3, 3), (1, 0), (3, 0), (0, 1), (0, 3), (0, 0))
STEPS = (
    [(0, 0, p) for p in range(8)]
    + [(0, 1, p) for p in range(3)]
    + [(1, 0, p) for p in range(2)]
    + [(0, 1, p) for p in range(3, 8)]
    + [(1, 0, p) for p in range(2, 8)]
    + [(1, 1, p) for p in range(8)]
)

def looked_up(table, at):
    found = jnp.int32(table[0])
    for i in range(1, len(table)):
        if table[i] != table[i - 1]:
            found = found + (table[i] - table[i - 1]) * jnp.where(at >= i, 1, 0)
    return found


def whole_kernel(
    scale,
    query_in,
    grad_in,
    position_hbm,
    offset_hbm,
    cache_in,
    first_in,
    second_in,
    slot_grad_out,
    query_grad_out,
    stage,
    first_out,
    second_out,
    position_in,
    offset_in,
    position_ref,
    offset_ref,
    q_all,
    g_all,
    key_ref,
    value_ref,
    key_t_ref,
    key_grad,
    value_grad,
    own_stats,
    stats_in,
    known,
    terms,
    terms_in,
    core_out,
    core_in,
    chip_out,
    chip_in,
    total_out,
    total_in,
    load_sem,
    gather_send,
    gather_recv,
    stats_send,
    stats_recv,
    known_send,
    known_recv,
    terms_send,
    terms_recv,
    conv_send,
    conv_recv,
):
    n_slot = SIDE * SIDE
    kv_count, slots, head_width = key_ref.shape
    group = q_all.shape[3]
    own_rows = q_all.shape[2]
    width = own_rows * group
    scale2 = scale * math.log2(math.e)
    me = lax.axis_index("slot")
    my_y, my_z = me // SIDE, me % SIDE
    conv = lax.axis_index("conv")
    core = conv % 2
    sibling = conv + 1 - 2 * core
    partner = (conv + 2) % 4

    def slot_at(y, z):
        return ((y + SIDE) % SIDE) * SIDE + (z + SIDE) % SIDE

    barrier = pltpu.get_barrier_semaphore()

    def greet(i, _):
        pl.semaphore_signal(barrier, inc=1, device_id={"slot": (me + i) % n_slot}, device_id_type=MESH)
        return 0

    lax.fori_loop(1, n_slot, greet, 0)
    pl.semaphore_signal(barrier, inc=1, device_id={"conv": sibling}, device_id_type=MESH)
    pl.semaphore_signal(barrier, inc=1, device_id={"conv": partner}, device_id_type=MESH)

    loads = []
    for i, (source, target) in enumerate(((query_in, q_all), (grad_in, g_all))):
        for k in range(kv_count):
            loads.append(pltpu.make_async_copy(source.at[:, k * group : (k + 1) * group, :], target.at[k, me], load_sem.at[i, k]))
    moments = [pltpu.make_async_copy(x, y, load_sem.at[2, 1 + i]) for i, (x, y) in enumerate(((first_in, first_out), (second_in, second_out)))]
    cache_load = pltpu.make_async_copy(cache_in, stage, load_sem.at[2, 0])
    for load in loads:
        load.start()
    cache_load.start()
    small = [pltpu.make_async_copy(x, y, load_sem.at[i, 2]) for i, (x, y) in enumerate(((position_hbm, position_in), (offset_hbm, offset_in)))]
    for load in small:
        load.start()
    for load in loads:
        load.wait()

    pl.semaphore_wait(barrier, n_slot + 1)

    def gather_copy(tensor, k, block, device):
        view = (q_all, g_all)[tensor].at[k, block]
        return pltpu.make_async_remote_copy(
            src_ref=view,
            dst_ref=view,
            send_sem=gather_send.at[tensor, k],
            recv_sem=gather_recv.at[tensor, k, block],
            device_id={"slot": device},
            device_id_type=MESH,
        )

    def ring(tensor, first, step):
        along_y = (tensor == 0) == first
        return slot_at(my_y + step, my_z) if along_y else slot_at(my_y, my_z + step)

    def gather_own(k):
        for first in (True, False):
            for tensor in (0, 1):
                for step in (1, -1, 2):
                    gather_copy(tensor, k, me, ring(tensor, first, step)).start()

    def gather_turn(k, relay=False):
        for step in (1, -1, 2):
            for tensor in (0, 1):
                gather_copy(tensor, k, ring(tensor, True, step), me).wait_recv()
                if relay:
                    gather_relay(k, (tensor,), (step,))

    def gather_relay(k, tensors=(0, 1), steps=(1, -1, 2)):
        for step in steps:
            for tensor in tensors:
                block = ring(tensor, True, step)
                for onward in (1, -1, 2):
                    gather_copy(tensor, k, block, ring(tensor, False, onward)).start()

    def gather_wait(k, dy, dz):
        for tensor, last in ((0, dz), (1, dy)):
            if last != 0:
                gather_copy(tensor, k, slot_at(my_y + dy, my_z + dz), me).wait_recv()

    gather_own(0)
    for load in moments:
        load.start()
    for load in small + [cache_load]:
        load.wait()
    for k in range(kv_count):
        key = stage[0, pl.ds(k, slots, stride=kv_count), :]
        key_ref[k] = key.astype(BF16)
        key_t_ref[k] = key.T.astype(BF16)
        value_ref[k] = stage[1, pl.ds(k, slots, stride=kv_count), :].astype(BF16)
    key_grad[...] = jnp.zeros_like(key_grad)
    value_grad[...] = jnp.zeros_like(value_grad)
    for i in range(slots // 128):
        row = offset_in[i : i + 1].astype(F32)
        offset_ref[i * 128 : (i + 1) * 128] = jnp.broadcast_to(row, (128, 128)).T
    spread = lax.broadcasted_iota(jnp.int32, (own_rows, width), 1) // group == lax.broadcasted_iota(jnp.int32, (own_rows, width), 0)
    for i in range(n_slot * own_rows // 128):
        rows = jnp.broadcast_to(position_in[i : i + 1].astype(F32), (128, 128)).T
        for j in range(128 // own_rows):
            mine = lanes(rows[j * own_rows : (j + 1) * own_rows], width)
            position_ref[i * (128 // own_rows) + j] = jnp.where(spread, mine, 0.0).sum(0, keepdims=True)

    def all_slots(k, source, target, send_sem, recv_sem, own_source):
        def send(i, _):
            other = (me + i) % n_slot
            pltpu.make_async_remote_copy(
                src_ref=source.at[k, me if own_source else other],
                dst_ref=target.at[k, me],
                send_sem=send_sem.at[k],
                recv_sem=recv_sem.at[k],
                device_id={"slot": other},
                device_id_type=MESH,
            ).start()
            return 0

        lax.fori_loop(1, n_slot, send, 0)

    def wait_all(k, ref, sem):
        view = ref.at[k, pl.ds(0, n_slot - 1)]
        pltpu.make_async_copy(view, view, sem.at[k]).wait()

    def stats_out(k):
        all_slots(k, own_stats, stats_in, stats_send, stats_recv, False)

    def stats_combine(k):
        wait_all(k, stats_in, stats_recv)
        stats_in[k, me] = own_stats[k, me]
        every = stats_in[k]
        top = every[:, 0:2].max(0)
        fade = jnp.exp2(every[:, 0:2] - top[None])
        total = (every[:, 2:4] * fade).sum(0)
        row_sum = (every[:, 4:6] * fade).sum(0) / total
        known[k, me, 0:2] = top + jnp.log2(total)
        known[k, me, 2:4] = row_sum
        all_slots(k, known, known, known_send, known_recv, True)

    def terms_copy(k, block):
        return pltpu.make_async_remote_copy(
            src_ref=terms.at[k, block],
            dst_ref=terms_in.at[k, me],
            send_sem=terms_send.at[k],
            recv_sem=terms_recv.at[k],
            device_id={"slot": block},
            device_id_type=MESH,
        )

    def terms_out(k, pair):
        for dy, dz in FAR_FIRST[2 * pair : 2 * pair + 2]:
            if (dy, dz) != (0, 0):
                terms_copy(k, slot_at(my_y + dy, my_z + dz)).start()

    def terms_end(k):
        wait_all(k, terms_in, terms_recv)

        def add(i, total):
            return total + terms_in[k, (me + i) % n_slot].astype(F32)

        total = lax.fori_loop(1, n_slot, add, terms[k, me].astype(F32))
        query_grad_out[:, k * group : (k + 1) * group, :] = total.T.reshape(own_rows, group, head_width)

    half = slots // 2

    def conv_copy(hop, k, i, device):
        source, target = ((core_out, core_in), (chip_out, chip_in), (total_out, total_in))[hop]
        return pltpu.make_async_remote_copy(
            src_ref=source.at[k, i],
            dst_ref=target.at[k, i],
            send_sem=conv_send.at[k, hop, i],
            recv_sem=conv_recv.at[k, hop, i],
            device_id={"conv": device},
            device_id_type=MESH,
        )

    def own_grad(k, i, owner):
        rows = pl.ds(pl.multiple_of(owner * half, half), half)
        return key_grad[k, rows, :] * scale if i == 0 else value_grad[k, rows, :]

    def store_total(k, i, owner, value):
        place = pl.ds(pl.multiple_of(owner * (half * kv_count), half * kv_count) + k, half, stride=kv_count)
        slot_grad_out[i, place, :] = value

    def conv_one(k):
        for i in (0, 1):
            core_out[k, i] = own_grad(k, i, 1 - core).astype(BF16)
            conv_copy(0, k, i, sibling).start()

    def conv_two(k):
        for i in (0, 1):
            conv_copy(0, k, i, sibling).wait_recv()
            chip_out[k, i] = (own_grad(k, i, core) + core_in[k, i].astype(F32)).astype(BF16)
            conv_copy(1, k, i, partner).start()

    def conv_three(k):
        for i in (0, 1):
            conv_copy(1, k, i, partner).wait_recv()
            total_out[k, i] = (chip_out[k, i].astype(F32) + chip_in[k, i].astype(F32)).astype(BF16)
            conv_copy(2, k, i, sibling).start()
            store_total(k, i, core, total_out[k, i].astype(F32))

    def conv_end(k):
        for i in (0, 1):
            conv_copy(2, k, i, sibling).wait_recv()
            store_total(k, i, 1 - core, total_in[k, i].astype(F32))
            for hop in range(3):
                conv_copy(hop, k, i, sibling).wait_send()

    def step(t, _):
        def at_step(at):
            return pl.when(t == at)

        for work, k, at in (
            (functools.partial(gather_turn, relay=True), 0, 0),
            (gather_own, 1, 0),
            (stats_out, 0, 8),
            (gather_turn, 1, 8),
            (stats_combine, 0, 11),
            (gather_relay, 1, 11),
            (stats_out, 1, 18),
            (stats_combine, 1, 21),
        ):

            @at_step(at)
            def _():
                work(k)

        for k, at in ((0, 11), (1, 24)):

            @at_step(at)
            def _():
                wait_all(k, known, known_recv)

        for at, (which, k, pair) in enumerate(STEPS):
            if which == 0:

                @at_step(at)
                def _():
                    for place in NEAR_FIRST[2 * pair : 2 * pair + 2]:
                        gather_wait(k, *place)

        for at, (which, k, pair) in enumerate(STEPS[:-1]):
            if which == 1:

                @at_step(at + 1)
                def _():
                    terms_out(k, pair)

        for work, at in ((conv_one, 24), (conv_two, 26)):

            @at_step(at)
            def _():
                work(0)

        which, k, pair = (looked_up([entry[i] for entry in STEPS], t) for i in range(3))

        def blocks_of(order):
            found = []
            for i in (0, 1):
                dy, dz = (looked_up([d[axis] for d in order[i::2]], pair) for axis in (0, 1))
                found.append(slot_at(my_y + dy, my_z + dz))
            return found

        def rows_of(ref, blocks):
            return jnp.concatenate([ref[k, block].reshape(width, head_width) for block in blocks], axis=0)

        def positions_of(blocks):
            return jnp.concatenate([position_ref[block] for block in blocks], axis=1)

        @pl.when(which == 0)
        def _():
            blocks = blocks_of(NEAR_FIRST)
            stats = stats_pass(
                rows_of(q_all, blocks),
                rows_of(g_all, blocks),
                key_ref.at[k],
                value_ref.at[k],
                offset_ref,
                positions_of(blocks),
                scale2,
                STATS_CHUNK,
            )
            for i, stat in enumerate(stats):
                for j in range(2 * width // 128):
                    row = i * (width // 128) + j % (width // 128)
                    own_stats[k, blocks[j * 128 // width], row : row + 1] = stat[:, j * 128 : (j + 1) * 128]

        @pl.when(which == 1)
        def _():
            blocks = blocks_of(FAR_FIRST)
            stats = [known[k, block] for block in blocks]
            both = [jnp.concatenate([stat[row : row + 1] for stat in stats for row in (i, i + 1)], axis=1) for i in (0, 2)]
            found = grad_pass(
                rows_of(q_all, blocks),
                rows_of(g_all, blocks),
                key_ref.at[k],
                value_ref.at[k],
                key_t_ref.at[k],
                offset_ref,
                positions_of(blocks),
                both[0],
                both[1],
                key_grad.at[k],
                value_grad.at[k],
                scale2,
                GRADS_CHUNK,
            )
            found = (found * scale).astype(BF16)
            for i, block in enumerate(blocks):
                terms[k, block] = found[:, i * width : (i + 1) * width]

        return 0

    lax.fori_loop(0, len(STEPS), step, 0)
    terms_out(*STEPS[-1][1:])
    conv_one(1)
    conv_three(0)
    conv_two(1)
    terms_end(0)
    conv_end(0)
    terms_end(1)
    conv_three(1)
    for k in range(kv_count):
        for tensor, buffer in enumerate((q_all, g_all)):
            view = buffer.at[k, pl.ds(0, n_slot - 1)]
            pltpu.make_async_copy(view, view, gather_send.at[tensor, k]).wait()
        wait_all(k, own_stats, stats_send)
        wait_all(k, known, known_send)
        wait_all(k, terms, terms_send)
    for load in moments:
        load.wait()
    conv_end(1)


def local(queries, out_grad, row_positions, slot_offsets, cache, first_moment, second_moment):
    own_rows, head_count, head_width = queries.shape
    kv_count, slots = cache.shape[2], cache.shape[1]
    group = head_count // kv_count
    blocks = row_positions.shape[0] // own_rows
    width = own_rows * group
    scale = 1.0 / math.sqrt(head_width)

    flat = (2, slots * kv_count, head_width)

    vmem = pl.BlockSpec(memory_space=pltpu.VMEM)
    hbm = pl.BlockSpec(memory_space=pltpu.HBM)
    dma = pltpu.SemaphoreType.DMA
    rows_all = pltpu.VMEM((kv_count, blocks, own_rows, group, head_width), BF16)
    in_hbm = lambda x: pltpu.with_memory_space_constraint(x, pltpu.HBM)
    slots_half = pltpu.VMEM((kv_count, slots, head_width), BF16)
    slots_full = pltpu.VMEM((kv_count, slots, head_width), F32)
    stats = pltpu.VMEM((kv_count, blocks, 8, 128), F32)
    conv_half = pltpu.VMEM((kv_count, 2, slots // 2, head_width), BF16)
    slot_grad, query_grad, cache_flat, first_flat, second_flat = pl.pallas_call(
        functools.partial(whole_kernel, scale),
        out_shape=(jax.ShapeDtypeStruct(flat, F32), jax.ShapeDtypeStruct(queries.shape, F32)) + (jax.ShapeDtypeStruct(flat, F32),) * 3,
        in_specs=[hbm] * 7,
        out_specs=(vmem,) * 5,
        scratch_shapes=[
            pltpu.VMEM((blocks * own_rows // 128, 128), jnp.int32),
            pltpu.VMEM((slots // 128, 128), jnp.int32),
            pltpu.VMEM((blocks, 1, width), F32),
            pltpu.VMEM((slots, 128), F32),
            rows_all,
            rows_all,
            slots_half,
            slots_half,
            pltpu.VMEM((kv_count, head_width, slots), BF16),
            slots_full,
            slots_full,
            stats,
            stats,
            stats,
            pltpu.VMEM((kv_count, blocks, head_width, width), BF16),
            pltpu.VMEM((kv_count, blocks, head_width, width), BF16),
        ]
        + [conv_half] * 6
        + [
            dma((3, 4)),
            dma((2, kv_count)),
            dma((2, kv_count, blocks)),
            dma((kv_count,)),
            dma((kv_count,)),
            dma((kv_count,)),
            dma((kv_count,)),
            dma((kv_count,)),
            dma((kv_count,)),
            dma((kv_count, 3, 2)),
            dma((kv_count, 3, 2)),
        ],
        compiler_params=pltpu.CompilerParams(collective_id=0, has_side_effects=True, vmem_limit_bytes=36 << 20),
        name="whole",
    )(in_hbm(queries), in_hbm(out_grad), in_hbm(row_positions.reshape(-1, 128)), in_hbm(slot_offsets.reshape(-1, 128)), *(in_hbm(x.reshape(flat)) for x in (cache, first_moment, second_moment)))

    new_first = beta_one * first_flat + (1.0 - beta_one) * slot_grad
    new_second = beta_two * second_flat + (1.0 - beta_two) * slot_grad * slot_grad
    first_fix = 1.0 - beta_one**STEP
    second_fix = 1.0 - beta_two**STEP
    new_cache = cache_flat - learn_rate * (new_first / first_fix) / (jnp.sqrt(new_second / second_fix) + adam_eps)
    return tuple(x.reshape(cache.shape) for x in (new_cache, new_first, new_second)) + (query_grad,)


def solution(mesh):
    rows = P(("conv", "slot"), "head", None)
    slots = P(None, "slot", "head", None)
    return jax.shard_map(
        local,
        mesh=mesh,
        in_specs=(rows, rows, P("conv"), P("slot"), slots, slots, slots),
        out_specs=(slots, slots, slots, rows),
        check_vma=False,
    )
```

```python
import functools
import math

import jax
import jax.numpy as jnp
from jax import lax
from jax.experimental import pallas as pl
from jax.experimental.pallas import tpu as pltpu
from jax.sharding import PartitionSpec as P

STEP = 20

SIDE = 4
STATS_CHUNK = 256
GRADS_CHUNK = 256

learn_rate = 0.01
beta_one = 0.9
beta_two = 0.95
adam_eps = 1e-08
masked_score = -1e30

MESH = pl.DeviceIdType.MESH
BF16 = jnp.bfloat16
F32 = jnp.float32


def nt(a, b):
    return lax.dot_general(a, b, (((1,), (1,)), ((), ())), preferred_element_type=F32)


def nn(a, b):
    return lax.dot_general(a, b, (((1,), (0,)), ((), ())), preferred_element_type=F32)


def lanes(column, width):
    return jnp.concatenate([column] * (width // column.shape[1]), axis=1)


def stats_pass(q, g, key_ref, value_ref, offset_ref, position, score_scale, chunk):
    width = q.shape[0]
    largest = jnp.full((8, width), masked_score, F32)
    total = jnp.zeros((8, width), F32)
    product = jnp.zeros((8, width), F32)
    for at in range(0, key_ref.shape[0], chunk):
        score = nt(key_ref[at : at + chunk], q)
        prob_grad = nt(value_ref[at : at + chunk], g)
        visible = lanes(offset_ref[at : at + chunk], width) <= position
        score = jnp.where(visible, score * score_scale, masked_score).reshape(chunk // 8, 8, width)
        now = jnp.maximum(largest, score.max(0))
        weight = jnp.exp2(score - now[None])
        fade = jnp.exp2(largest - now)
        total = total * fade + weight.sum(0)
        product = product * fade + (weight * prob_grad.reshape(chunk // 8, 8, width)).sum(0)
        largest = now
    top = largest.max(0, keepdims=True)
    fade = jnp.exp2(largest - top)
    return top, (total * fade).sum(0, keepdims=True), (product * fade).sum(0, keepdims=True)


def grad_pass(q, g, key_ref, value_ref, key_t_ref, offset_ref, position, log_total, row_sum, key_grad, value_grad, score_scale, chunk):
    width = q.shape[0]
    query_grad = jnp.zeros((q.shape[1], width), F32)
    for at in range(0, key_ref.shape[0], chunk):
        part = slice(at, at + chunk)
        score = nt(key_ref[part], q)
        prob_grad = nt(value_ref[part], g)
        visible = lanes(offset_ref[part], width) <= position
        probability = jnp.where(visible, jnp.exp2(score * score_scale - log_total), 0.0)
        score_grad = (probability * (prob_grad - row_sum)).astype(BF16)
        value_grad[part] += nn(probability.astype(BF16), g)
        key_grad[part] += nn(score_grad, q)
        query_grad = query_grad + nn(key_t_ref[:, part], score_grad)
    return query_grad


NEAR_FIRST = ((0, 0), (0, 1), (0, 3), (1, 0), (3, 0), (0, 2), (2, 0), (1, 1), (1, 3), (3, 1), (3, 3), (2, 1), (2, 3), (1, 2), (3, 2), (2, 2))
FAR_FIRST = ((2, 2), (2, 1), (1, 2), (2, 3), (3, 2), (2, 0), (0, 2), (1, 1), (1, 3), (3, 1), (3, 3), (1, 0), (3, 0), (0, 1), (0, 3), (0, 0))
STEPS = (
    [(0, 0, p) for p in range(8)]
    + [(0, 1, p) for p in range(3)]
    + [(1, 0, p) for p in range(2)]
    + [(0, 1, p) for p in range(3, 8)]
    + [(1, 0, p) for p in range(2, 8)]
    + [(1, 1, p) for p in range(8)]
)
REDUCE = (
    ((0, 2, 2), (1, 2, 2), (1, 1, 2)),
    ((0, 1, 2), (1, 3, 2)),
    ((0, 3, 2), (0, 2, 1), (0, 2, 3), (1, 0, 2), (1, 2, 1), (1, 2, 3)),
    ((0, 0, 2), (0, 1, 1), (1, 1, 1)),
    ((0, 1, 3), (0, 3, 1), (0, 2, 0), (1, 1, 3), (1, 3, 1), (1, 2, 0)),
    ((0, 3, 3), (1, 3, 3), (1, 0, 1)),
    ((0, 0, 1), (0, 1, 0), (1, 0, 3), (1, 1, 0)),
    ((0, 0, 3), (0, 3, 0), (1, 3, 0)),
    (),
    ((0, 0, 0), (1, 0, 0)),
)
REDUCE_AT = ((13, 15, 19, 20, 21, 22, 23, 24, 25, 26), (25, 26, 27, 28, 29, 30, 31))


def looked_up(table, at):
    found = jnp.int32(table[0])
    for i in range(1, len(table)):
        if table[i] != table[i - 1]:
            found = found + (table[i] - table[i - 1]) * jnp.where(at >= i, 1, 0)
    return found


def whole_kernel(
    scale,
    query_in,
    grad_in,
    position_hbm,
    offset_hbm,
    cache_in,
    first_in,
    second_in,
    slot_grad_out,
    query_grad_out,
    stage,
    first_out,
    second_out,
    position_in,
    offset_in,
    position_ref,
    offset_ref,
    q_all,
    g_all,
    key_ref,
    value_ref,
    key_t_ref,
    key_grad,
    value_grad,
    own_stats,
    stats_in,
    known,
    terms,
    far_one,
    near_one,
    far_two,
    near_two,
    core_out,
    core_in,
    chip_out,
    chip_in,
    total_out,
    total_in,
    load_sem,
    gather_send,
    gather_recv,
    stats_send,
    stats_recv,
    known_send,
    known_recv,
    reduce_send,
    far_one_recv,
    near_one_recv,
    far_two_recv,
    near_two_recv,
    conv_send,
    conv_recv,
):
    n_slot = SIDE * SIDE
    kv_count, slots, head_width = key_ref.shape
    group = q_all.shape[3]
    own_rows = q_all.shape[2]
    width = own_rows * group
    scale2 = scale * math.log2(math.e)
    me = lax.axis_index("slot")
    my_y, my_z = me // SIDE, me % SIDE
    conv = lax.axis_index("conv")
    core = conv % 2
    sibling = conv + 1 - 2 * core
    partner = (conv + 2) % 4

    def slot_at(y, z):
        return ((y + SIDE) % SIDE) * SIDE + (z + SIDE) % SIDE

    barrier = pltpu.get_barrier_semaphore()

    def greet(i, _):
        pl.semaphore_signal(barrier, inc=1, device_id={"slot": (me + i) % n_slot}, device_id_type=MESH)
        return 0

    lax.fori_loop(1, n_slot, greet, 0)
    pl.semaphore_signal(barrier, inc=1, device_id={"conv": sibling}, device_id_type=MESH)
    pl.semaphore_signal(barrier, inc=1, device_id={"conv": partner}, device_id_type=MESH)

    loads = []
    for i, (source, target) in enumerate(((query_in, q_all), (grad_in, g_all))):
        for k in range(kv_count):
            loads.append(pltpu.make_async_copy(source.at[:, k * group : (k + 1) * group, :], target.at[k, me], load_sem.at[i, k]))
    moments = [pltpu.make_async_copy(x, y, load_sem.at[2, 1 + i]) for i, (x, y) in enumerate(((first_in, first_out), (second_in, second_out)))]
    cache_load = pltpu.make_async_copy(cache_in, stage, load_sem.at[2, 0])
    for load in loads:
        load.start()
    cache_load.start()
    small = [pltpu.make_async_copy(x, y, load_sem.at[i, 2]) for i, (x, y) in enumerate(((position_hbm, position_in), (offset_hbm, offset_in)))]
    for load in small:
        load.start()
    for load in loads:
        load.wait()

    pl.semaphore_wait(barrier, n_slot + 1)

    def gather_copy(tensor, k, block, device):
        view = (q_all, g_all)[tensor].at[k, block]
        return pltpu.make_async_remote_copy(
            src_ref=view,
            dst_ref=view,
            send_sem=gather_send.at[tensor, k],
            recv_sem=gather_recv.at[tensor, k, block],
            device_id={"slot": device},
            device_id_type=MESH,
        )

    def ring(tensor, first, step):
        along_y = (tensor == 0) == first
        return slot_at(my_y + step, my_z) if along_y else slot_at(my_y, my_z + step)

    def gather_own(k):
        for first in (True, False):
            for tensor in (0, 1):
                for step in (1, -1, 2):
                    gather_copy(tensor, k, me, ring(tensor, first, step)).start()

    def gather_turn(k, relay=False):
        for step in (1, -1, 2):
            for tensor in (0, 1):
                gather_copy(tensor, k, ring(tensor, True, step), me).wait_recv()
                if relay:
                    gather_relay(k, (tensor,), (step,))

    def gather_relay(k, tensors=(0, 1), steps=(1, -1, 2)):
        for step in steps:
            for tensor in tensors:
                block = ring(tensor, True, step)
                for onward in (1, -1, 2):
                    gather_copy(tensor, k, block, ring(tensor, False, onward)).start()

    def gather_wait(k, dy, dz):
        for tensor, last in ((0, dz), (1, dy)):
            if last != 0:
                gather_copy(tensor, k, slot_at(my_y + dy, my_z + dz), me).wait_recv()

    gather_own(0)
    for load in moments:
        load.start()
    for load in small + [cache_load]:
        load.wait()
    for k in range(kv_count):
        key = stage[0, pl.ds(k, slots, stride=kv_count), :]
        key_ref[k] = key.astype(BF16)
        key_t_ref[k] = key.T.astype(BF16)
        value_ref[k] = stage[1, pl.ds(k, slots, stride=kv_count), :].astype(BF16)
    key_grad[...] = jnp.zeros_like(key_grad)
    value_grad[...] = jnp.zeros_like(value_grad)
    for i in range(slots // 128):
        row = offset_in[i : i + 1].astype(F32)
        offset_ref[i * 128 : (i + 1) * 128] = jnp.broadcast_to(row, (128, 128)).T
    spread = lax.broadcasted_iota(jnp.int32, (own_rows, width), 1) // group == lax.broadcasted_iota(jnp.int32, (own_rows, width), 0)
    for i in range(n_slot * own_rows // 128):
        rows = jnp.broadcast_to(position_in[i : i + 1].astype(F32), (128, 128)).T
        for j in range(128 // own_rows):
            mine = lanes(rows[j * own_rows : (j + 1) * own_rows], width)
            position_ref[i * (128 // own_rows) + j] = jnp.where(spread, mine, 0.0).sum(0, keepdims=True)

    def all_slots(k, source, target, send_sem, recv_sem, own_source):
        def send(i, _):
            other = (me + i) % n_slot
            pltpu.make_async_remote_copy(
                src_ref=source.at[k, me if own_source else other],
                dst_ref=target.at[k, me],
                send_sem=send_sem.at[k],
                recv_sem=recv_sem.at[k],
                device_id={"slot": other},
                device_id_type=MESH,
            ).start()
            return 0

        lax.fori_loop(1, n_slot, send, 0)

    def wait_all(k, ref, sem):
        view = ref.at[k, pl.ds(0, n_slot - 1)]
        pltpu.make_async_copy(view, view, sem.at[k]).wait()

    def stats_out(k):
        all_slots(k, own_stats, stats_in, stats_send, stats_recv, False)

    def stats_combine(k):
        wait_all(k, stats_in, stats_recv)
        stats_in[k, me] = own_stats[k, me]
        every = stats_in[k]
        top = every[:, 0:2].max(0)
        fade = jnp.exp2(every[:, 0:2] - top[None])
        total = (every[:, 2:4] * fade).sum(0)
        row_sum = (every[:, 4:6] * fade).sum(0) / total
        known[k, me, 0:2] = top + jnp.log2(total)
        known[k, me, 2:4] = row_sum
        all_slots(k, known, known, known_send, known_recv, True)

    def reduce_copy(color, k, source, target, recv_sem, device):
        return pltpu.make_async_remote_copy(
            src_ref=source,
            dst_ref=target,
            send_sem=reduce_send.at[k, color],
            recv_sem=recv_sem,
            device_id={"slot": device},
            device_id_type=MESH,
        )

    quarter = head_width // 4

    def reduce_event(k, color, da, db):
        dy, dz = (da, db) if color == 0 else (db, da)
        block = slot_at(my_y + dy, my_z + dz)
        a_at = ((my_y if color == 0 else my_z) + da) % SIDE
        mine = terms.at[k, color, block]

        def arrived(target, sem):
            pltpu.make_async_copy(target, target, sem).wait()
            return target[...].astype(F32)

        def add(side, target, sem):
            rows = pl.ds(side * quarter, quarter)
            mine[rows] = (mine[rows].astype(F32) + arrived(target, sem)).astype(BF16)

        def pieces(target, sems, first, index):
            for side, step in ((0, 1), (1, -1)):
                place = (k, color, side) + index
                rows = mine.at[pl.ds(side * quarter, quarter)]
                reduce_copy(color, k, rows, target.at[place], sems.at[place], ring(color, first, step)).start()

        def onward(target, sems, first, index, side):
            place = (k, color, side) + index
            reduce_copy(color, k, mine, target.at[place], sems.at[place], ring(color, first, 1 - 2 * side)).start()

        if db == 2:
            pieces(far_one, far_one_recv, False, (a_at,))
        elif db != 0:
            side = db // 2
            place = (k, color, side, a_at)
            add(side, far_one.at[place], far_one_recv.at[place])
            onward(near_one, near_one_recv, False, (a_at,), side)
        else:
            total = mine[...].astype(F32)
            for side in (0, 1):
                place = (k, color, side, a_at)
                total = total + arrived(near_one.at[place], near_one_recv.at[place])
            mine[...] = total.astype(BF16)
            if da == 2:
                pieces(far_two, far_two_recv, True, ())
            elif da != 0:
                side = da // 2
                place = (k, color, side)
                add(side, far_two.at[place], far_two_recv.at[place])
                onward(near_two, near_two_recv, True, (), side)

    def reduce_stage(k, stage):
        for event in REDUCE[stage]:
            reduce_event(k, *event)

    def reduce_end(k):
        sums = []
        for color in (0, 1):
            total = terms[k, color, me].astype(F32)
            for side in (0, 1):
                place = (k, color, side)
                view = near_two.at[place]
                pltpu.make_async_copy(view, view, near_two_recv.at[place]).wait()
                total = total + view[...].astype(F32)
            sums.append(total)
        rows = jnp.concatenate(sums, axis=0).T.reshape(own_rows, group, head_width)
        query_grad_out[:, k * group : (k + 1) * group, :] = rows

    half = slots // 2

    def conv_copy(hop, k, i, device):
        source, target = ((core_out, core_in), (chip_out, chip_in), (total_out, total_in))[hop]
        return pltpu.make_async_remote_copy(
            src_ref=source.at[k, i],
            dst_ref=target.at[k, i],
            send_sem=conv_send.at[k, hop, i],
            recv_sem=conv_recv.at[k, hop, i],
            device_id={"conv": device},
            device_id_type=MESH,
        )

    def own_grad(k, i, owner):
        rows = pl.ds(pl.multiple_of(owner * half, half), half)
        return key_grad[k, rows, :] * scale if i == 0 else value_grad[k, rows, :]

    def store_total(k, i, owner, value):
        place = pl.ds(pl.multiple_of(owner * (half * kv_count), half * kv_count) + k, half, stride=kv_count)
        slot_grad_out[i, place, :] = value

    def conv_one(k):
        for i in (0, 1):
            core_out[k, i] = own_grad(k, i, 1 - core).astype(BF16)
            conv_copy(0, k, i, sibling).start()

    def conv_two(k):
        for i in (0, 1):
            conv_copy(0, k, i, sibling).wait_recv()
            chip_out[k, i] = (own_grad(k, i, core) + core_in[k, i].astype(F32)).astype(BF16)
            conv_copy(1, k, i, partner).start()

    def conv_three(k):
        for i in (0, 1):
            conv_copy(1, k, i, partner).wait_recv()
            total_out[k, i] = (chip_out[k, i].astype(F32) + chip_in[k, i].astype(F32)).astype(BF16)
            conv_copy(2, k, i, sibling).start()
            store_total(k, i, core, total_out[k, i].astype(F32))

    def conv_end(k):
        for i in (0, 1):
            conv_copy(2, k, i, sibling).wait_recv()
            store_total(k, i, 1 - core, total_in[k, i].astype(F32))
            for hop in range(3):
                conv_copy(hop, k, i, sibling).wait_send()

    def step(t, _):
        def at_step(at):
            return pl.when(t == at)

        for work, k, at in (
            (functools.partial(gather_turn, relay=True), 0, 0),
            (gather_own, 1, 0),
            (stats_out, 0, 8),
            (gather_turn, 1, 8),
            (stats_combine, 0, 11),
            (gather_relay, 1, 11),
            (stats_out, 1, 18),
            (stats_combine, 1, 21),
        ):

            @at_step(at)
            def _():
                work(k)

        for k, at in ((0, 11), (1, 24)):

            @at_step(at)
            def _():
                wait_all(k, known, known_recv)

        for at, (which, k, pair) in enumerate(STEPS):
            if which == 0:

                @at_step(at)
                def _():
                    for place in NEAR_FIRST[2 * pair : 2 * pair + 2]:
                        gather_wait(k, *place)

        for stage, at in enumerate(REDUCE_AT[0]):
            also = REDUCE_AT[1][stage] if stage < len(REDUCE_AT[1]) else at

            @pl.when((t == at) | (t == also))
            def _():
                reduce_stage(jnp.where(t == at, 0, 1), stage)

        for work, at in ((conv_one, 24), (conv_two, 26)):

            @at_step(at)
            def _():
                work(0)

        which, k, pair = (looked_up([entry[i] for entry in STEPS], t) for i in range(3))

        def blocks_of(order):
            found = []
            for i in (0, 1):
                dy, dz = (looked_up([d[axis] for d in order[i::2]], pair) for axis in (0, 1))
                found.append(slot_at(my_y + dy, my_z + dz))
            return found

        def rows_of(ref, blocks):
            return jnp.concatenate([ref[k, block].reshape(width, head_width) for block in blocks], axis=0)

        def positions_of(blocks):
            return jnp.concatenate([position_ref[block] for block in blocks], axis=1)

        @pl.when(which == 0)
        def _():
            blocks = blocks_of(NEAR_FIRST)
            stats = stats_pass(
                rows_of(q_all, blocks),
                rows_of(g_all, blocks),
                key_ref.at[k],
                value_ref.at[k],
                offset_ref,
                positions_of(blocks),
                scale2,
                STATS_CHUNK,
            )
            for i, stat in enumerate(stats):
                for j in range(2 * width // 128):
                    row = i * (width // 128) + j % (width // 128)
                    own_stats[k, blocks[j * 128 // width], row : row + 1] = stat[:, j * 128 : (j + 1) * 128]

        @pl.when(which == 1)
        def _():
            blocks = blocks_of(FAR_FIRST)
            stats = [known[k, block] for block in blocks]
            both = [jnp.concatenate([stat[row : row + 1] for stat in stats for row in (i, i + 1)], axis=1) for i in (0, 2)]
            found = grad_pass(
                rows_of(q_all, blocks),
                rows_of(g_all, blocks),
                key_ref.at[k],
                value_ref.at[k],
                key_t_ref.at[k],
                offset_ref,
                positions_of(blocks),
                both[0],
                both[1],
                key_grad.at[k],
                value_grad.at[k],
                scale2,
                GRADS_CHUNK,
            )
            found = (found * scale).astype(BF16)
            for i, block in enumerate(blocks):
                for color in (0, 1):
                    terms[k, color, block] = found[color * head_width // 2 : (color + 1) * head_width // 2, i * width : (i + 1) * width]

        return 0

    lax.fori_loop(0, len(STEPS), step, 0)
    conv_one(1)
    conv_three(0)
    conv_two(1)
    reduce_stage(1, 7)
    reduce_end(0)
    conv_end(0)
    reduce_stage(1, 8)
    reduce_stage(1, 9)
    conv_three(1)
    reduce_end(1)
    for k in range(kv_count):
        for tensor, buffer in enumerate((q_all, g_all)):
            view = buffer.at[k, pl.ds(0, n_slot - 1)]
            pltpu.make_async_copy(view, view, gather_send.at[tensor, k]).wait()
        wait_all(k, own_stats, stats_send)
        wait_all(k, known, known_send)
        for color in (0, 1):
            view = terms.at[k, color, pl.ds(0, n_slot - 1)]
            pltpu.make_async_copy(view, view, reduce_send.at[k, color]).wait()
    for load in moments:
        load.wait()
    conv_end(1)


def local(queries, out_grad, row_positions, slot_offsets, cache, first_moment, second_moment):
    own_rows, head_count, head_width = queries.shape
    kv_count, slots = cache.shape[2], cache.shape[1]
    group = head_count // kv_count
    blocks = row_positions.shape[0] // own_rows
    width = own_rows * group
    scale = 1.0 / math.sqrt(head_width)

    flat = (2, slots * kv_count, head_width)

    vmem = pl.BlockSpec(memory_space=pltpu.VMEM)
    hbm = pl.BlockSpec(memory_space=pltpu.HBM)
    dma = pltpu.SemaphoreType.DMA
    rows_all = pltpu.VMEM((kv_count, blocks, own_rows, group, head_width), BF16)
    in_hbm = lambda x: pltpu.with_memory_space_constraint(x, pltpu.HBM)
    slots_half = pltpu.VMEM((kv_count, slots, head_width), BF16)
    slots_full = pltpu.VMEM((kv_count, slots, head_width), F32)
    stats = pltpu.VMEM((kv_count, blocks, 8, 128), F32)
    conv_half = pltpu.VMEM((kv_count, 2, slots // 2, head_width), BF16)
    slot_grad, query_grad, cache_flat, first_flat, second_flat = pl.pallas_call(
        functools.partial(whole_kernel, scale),
        out_shape=(jax.ShapeDtypeStruct(flat, F32), jax.ShapeDtypeStruct(queries.shape, F32)) + (jax.ShapeDtypeStruct(flat, F32),) * 3,
        in_specs=[hbm] * 7,
        out_specs=(vmem,) * 5,
        scratch_shapes=[
            pltpu.VMEM((blocks * own_rows // 128, 128), jnp.int32),
            pltpu.VMEM((slots // 128, 128), jnp.int32),
            pltpu.VMEM((blocks, 1, width), F32),
            pltpu.VMEM((slots, 128), F32),
            rows_all,
            rows_all,
            slots_half,
            slots_half,
            pltpu.VMEM((kv_count, head_width, slots), BF16),
            slots_full,
            slots_full,
            stats,
            stats,
            stats,
            pltpu.VMEM((kv_count, 2, blocks, head_width // 2, width), BF16),
            pltpu.VMEM((kv_count, 2, 2, SIDE, head_width // 4, width), BF16),
            pltpu.VMEM((kv_count, 2, 2, SIDE, head_width // 2, width), BF16),
            pltpu.VMEM((kv_count, 2, 2, head_width // 4, width), BF16),
            pltpu.VMEM((kv_count, 2, 2, head_width // 2, width), BF16),
        ]
        + [conv_half] * 6
        + [
            dma((3, 4)),
            dma((2, kv_count)),
            dma((2, kv_count, blocks)),
            dma((kv_count,)),
            dma((kv_count,)),
            dma((kv_count,)),
            dma((kv_count,)),
            dma((kv_count, 2)),
            dma((kv_count, 2, 2, SIDE)),
            dma((kv_count, 2, 2, SIDE)),
            dma((kv_count, 2, 2)),
            dma((kv_count, 2, 2)),
            dma((kv_count, 3, 2)),
            dma((kv_count, 3, 2)),
        ],
        compiler_params=pltpu.CompilerParams(collective_id=0, has_side_effects=True, vmem_limit_bytes=34 << 20),
        name="whole",
    )(in_hbm(queries), in_hbm(out_grad), in_hbm(row_positions.reshape(-1, 128)), in_hbm(slot_offsets.reshape(-1, 128)), *(in_hbm(x.reshape(flat)) for x in (cache, first_moment, second_moment)))

    new_first = beta_one * first_flat + (1.0 - beta_one) * slot_grad
    new_second = beta_two * second_flat + (1.0 - beta_two) * slot_grad * slot_grad
    first_fix = 1.0 - beta_one**STEP
    second_fix = 1.0 - beta_two**STEP
    new_cache = cache_flat - learn_rate * (new_first / first_fix) / (jnp.sqrt(new_second / second_fix) + adam_eps)
    return tuple(x.reshape(cache.shape) for x in (new_cache, new_first, new_second)) + (query_grad,)


def solution(mesh):
    rows = P(("conv", "slot"), "head", None)
    slots = P(None, "slot", "head", None)
    return jax.shard_map(
        local,
        mesh=mesh,
        in_specs=(rows, rows, P("conv"), P("slot"), slots, slots, slots),
        out_specs=(slots, slots, slots, rows),
        check_vma=False,
    )
```
